32 devices in a mesh: scen: 2 (over x), hour: 4 (over z), reg: 4 (over y, core).
Axes of the slice: x: 2, y: 2, z: 4, core: 2. Of those that a mesh axis runs over, the one named last changes fastest.
Arguments:
- cost_rate: float32 [8, 672, 2048], P('scen', 'hour', 'reg'), may hold values from 0.05 to 1
- invest_cost: float32 [3, 2048], P(None, 'reg'), may hold values from 0.1 to 1
- tile: bfloat16 [4, 256, 2048], P('hour', None, 'reg'), may hold values from -0.1875 to 0.1875
- tile_mask: int32 [4, 256, 2048], P('hour', None, 'reg'), may hold values 0 or 1
- demand: float32 [8, 672, 256], P('scen', 'hour'), may hold values from -6 to 6
- dispatch: float32 [8, 672, 2048], P('scen', 'hour', 'reg'), may hold values from 0 to 1
- dual: float32 [8, 672, 256], P('scen', 'hour'), may hold values from 0 to 1
- cap_dual: float32 [8, 672, 2048], P('scen', 'hour', 'reg'), may hold values from 0 to 1
- capacity: float32 [8, 3, 2048], P('scen', None, 'reg'), may hold values from 0 to 2
- multiplier: float32 [8, 3, 2048], P('scen', None, 'reg'), may hold values from -3 to 3
- consensus: float32 [8, 3, 2048], P('scen', None, 'reg'), may hold values from 0 to 2
- scen_weight: float32 [8], P('scen'), may hold values from 0.1 to 1
- node_of: int32 [3, 8], P(None, 'scen'), may hold values from 0 to 3, as said below
Outputs:
- dispatch_out: float32 [8, 672, 2048], P('scen', 'hour', 'reg')
- dual_out: float32 [8, 672, 256], P('scen', 'hour', 'reg')
- capacity_out: float32 [8, 3, 2048], P('scen', None, 'reg')
- multiplier_out: float32 [8, 3, 2048], P('scen', None, 'reg')
The draws below stay inside these ranges and needn't reach their ends.
Inputs may be any that keep to these rules, and one draw needn't show every extreme that they name: `node_of`: at each section the nodes are runs of consecutive scenarios, numbered in order from 0; each node of a section lies within one node of the section before; section 0 is one node, the last section has 4 nodes, and node counts grow from section to section.
All inputs are finite; a program needn't handle non-finite values. No bound on the sum of `tile_mask` on one device may be relied on, other than what follows from the above.
Results may differ from the reference program's by a relative error of at most 0.0015.
Values may be sent and summed in bfloat16 or wider, within the bound.
No kernel may reach another device: no remote copies, remote signals or barrier semaphores. Data moves between devices by JAX's collectives and lax.ppermute only.
A program may use at most 64 MiB of HBM per device.

```python
import math
import jax
import jax.numpy as jnp
from jax import lax

COLS = 2048
CONS = 256
SECTIONS = 3
ITERS = 8
SCEN = 8
BLOCKS = 4
HOURS = 672
NODES = 4


def draw_node_of(key, part):
    shuffled = jax.random.permutation(key, SCEN - 1) + 1
    section_rows = []
    for section in range(SECTIONS):
        node_count = 1 + (NODES - 1) * section // (SECTIONS - 1)
        boundary = jnp.zeros((SCEN,), jnp.int32).at[shuffled[:node_count - 1]].add(1)
        section_rows.append(jnp.cumsum(boundary))
    return jnp.stack(section_rows).astype(jnp.int32)


def with_ends(drawn, key, smallest, top_value):
    longest = drawn.shape.index(max(drawn.shape))
    spots = []
    for shift in (0, 1):
        where = [jax.random.randint(jax.random.fold_in(key, axis), (), 0, length) for axis, length in enumerate(drawn.shape)]
        where[longest] = (where[longest] + shift) % drawn.shape[longest]
        spots.append(tuple(where))
    return drawn.at[spots[0]].set(smallest).at[spots[1]].set(top_value)


def levels(stream_key, extent, pieces, least, high):
    factor_of = 1.0
    for axis_at, parts in pieces:
        steps = jax.random.uniform(jax.random.fold_in(jax.random.fold_in(stream_key, 6), axis_at), (parts,), jnp.float32, least / len(pieces), high / len(pieces))
        factor_of = factor_of * jnp.repeat(jnp.exp(steps), extent[axis_at] // parts).reshape((-1,) + (1,) * (len(extent) - 1 - axis_at))
    return factor_of


def bell_draw(own_key, shape, deviation, limit, split=(), kind=jnp.bfloat16):
    level = levels(own_key, shape, split, -0.22, 0.18) if split else 1.0
    entries = jax.random.normal(own_key, shape, jnp.float32) * deviation * level
    return jnp.minimum(jnp.maximum(entries, -limit), limit).astype(kind)


def setup_inputs(seed: int = 0) -> dict:
    streams_of = jax.random.split(jax.random.key(seed), 14)
    return {
        "cost_rate": jnp.clip(jnp.exp(math.log(1.0) - 2.9957323 * jax.random.uniform(streams_of[0], (SCEN, HOURS, COLS), jnp.float32) ** levels(streams_of[0], (SCEN, HOURS, COLS), ((0, 2), (1, 4), (2, 4)), -0.2, 0.2)), 0.05, 1.0),
        "invest_cost": jnp.clip(jnp.exp(math.log(1.0) - 2.3025851 * jax.random.uniform(streams_of[1], (SECTIONS, COLS), jnp.float32) ** levels(streams_of[1], (SECTIONS, COLS), ((1, 4),), -0.2, 0.2)), 0.1, 1.0),
        "tile": bell_draw(streams_of[2], (BLOCKS, CONS, COLS), (COLS // 2) ** -0.5, 0.1875, ((0, 4), (2, 4))),
        "tile_mask": with_ends((jax.random.randint(streams_of[3], (BLOCKS, CONS, COLS), 0, 2) < 1).astype(jnp.int32), jax.random.fold_in(streams_of[3], 1), 0, 1),
        "demand": bell_draw(streams_of[4], (SCEN, HOURS, CONS), 1.0, 6.0, ((0, 2), (1, 4)), jnp.float32),
        "dispatch": jnp.clip(1.0 * jax.random.uniform(streams_of[5], (SCEN, HOURS, COLS), jnp.float32) ** levels(streams_of[5], (SCEN, HOURS, COLS), ((0, 2), (1, 4), (2, 4)), -0.2, 0.2), 0.0, 1.0),
        "dual": jnp.clip(1.0 * jax.random.uniform(streams_of[6], (SCEN, HOURS, CONS), jnp.float32) ** levels(streams_of[6], (SCEN, HOURS, CONS), ((0, 2), (1, 4)), -0.2, 0.2), 0.0, 1.0),
        "cap_dual": jnp.clip(1.0 * jax.random.uniform(streams_of[7], (SCEN, HOURS, COLS), jnp.float32) ** levels(streams_of[7], (SCEN, HOURS, COLS), ((0, 2), (1, 4), (2, 4)), -0.2, 0.2), 0.0, 1.0),
        "capacity": jnp.clip(2.0 * jax.random.uniform(streams_of[8], (SCEN, SECTIONS, COLS), jnp.float32) ** levels(streams_of[8], (SCEN, SECTIONS, COLS), ((0, 2), (2, 4)), -0.2, 0.2), 0.0, 2.0),
        "multiplier": bell_draw(streams_of[9], (SCEN, SECTIONS, COLS), 0.5, 3.0, ((0, 2), (2, 4)), jnp.float32),
        "consensus": jnp.clip(2.0 * jax.random.uniform(streams_of[10], (SCEN, SECTIONS, COLS), jnp.float32) ** levels(streams_of[10], (SCEN, SECTIONS, COLS), ((0, 2), (2, 4)), -0.2, 0.2), 0.0, 2.0),
        "scen_weight": jnp.clip(jnp.exp(math.log(1.0) - 2.3025851 * jax.random.uniform(streams_of[11], (SCEN,), jnp.float32) ** levels(streams_of[11], (SCEN,), ((0, 2),), -0.2, 0.2)), 0.1, 1.0),
        "node_of": draw_node_of(jax.random.fold_in(streams_of[13], 71), 0),
    }


RAMP_WEIGHT = 0.5
PENALTY = 1.0
STEP_PRIMAL = 0.3
STEP_INVEST = 0.5
STEP_DUAL = 0.3
STEP_CAP = 0.05


def reference(cost_rate, invest_cost, tile, tile_mask, demand, dispatch, dual, cap_dual, capacity, multiplier, consensus, scen_weight, node_of):
    matrix = tile * tile_mask.astype(jnp.bfloat16)
    matrix_wide = matrix.astype(jnp.float32)
    nscen = dispatch.shape[0]
    nhours = dispatch.shape[1]
    nblocks = tile.shape[0]
    nblock_hours = nhours // nblocks
    primal = dispatch
    dual_var = dual
    cap_var = cap_dual
    invest = capacity
    for step_index in range(ITERS):
        dual_low = lax.optimization_barrier(dual_var.astype(jnp.bfloat16)).astype(jnp.float32)
        dual_four = dual_low.reshape(nscen, nblocks, nblock_hours, -1)
        pulled = jnp.einsum("sbhr,brc->sbhc", dual_four, matrix_wide).reshape(primal.shape)
        padded = jnp.pad(primal, ((0, 0), (1, 1), (0, 0)))
        rough = 2.0 * primal - padded[:, :-2] - padded[:, 2:]
        grad_x = cost_rate + RAMP_WEIGHT * rough - pulled + cap_var
        zmean = jnp.sum(cap_var, axis=1) / nhours
        grad_u = invest_cost[None] + multiplier + PENALTY * (invest - consensus) - zmean[:, None, :]
        primal_new = jnp.maximum(primal - STEP_PRIMAL * grad_x, 0.0)
        invest_new = jnp.maximum(invest - STEP_INVEST * grad_u, 0.0)
        primal_ext = 2.0 * primal_new - primal
        invest_ext = 2.0 * invest_new - invest
        ext_low = lax.optimization_barrier(primal_ext.astype(jnp.bfloat16)).astype(jnp.float32)
        ext_four = ext_low.reshape(nscen, nblocks, nblock_hours, -1)
        image = jnp.einsum("sbhc,brc->sbhr", ext_four, matrix_wide).reshape(dual_var.shape)
        dual_var = jnp.maximum(dual_var + STEP_DUAL * (demand - image), 0.0)
        cap_var = jnp.maximum(cap_var + STEP_CAP * (primal_ext - jnp.sum(invest_ext, axis=1)[:, None, :]), 0.0)
        primal = primal_new
        invest = invest_new
    node_ids = jnp.arange(NODES, dtype=jnp.int32)
    one_hot = (node_of[:, :, None] == node_ids[None, None, :]).astype(jnp.float32)
    weighted = scen_weight[:, None, None] * invest
    node_sum = jnp.einsum("gsn,sgc->gnc", one_hot, weighted, precision=lax.Precision.HIGHEST)
    node_mass = jnp.einsum("gsn,s->gn", one_hot, scen_weight, precision=lax.Precision.HIGHEST)
    safe_mass = node_mass + (node_mass <= 0.0).astype(jnp.float32)
    average = node_sum / safe_mass[:, :, None]
    spread_back = jnp.einsum("gsn,gnc->sgc", one_hot, average, precision=lax.Precision.HIGHEST)
    multiplier_out = multiplier + PENALTY * (invest - spread_back)
    return (primal, dual_var, invest, multiplier_out)
```

```python
import functools

import jax
import jax.numpy as jnp
from jax import lax
from jax.experimental import pallas as pl
from jax.experimental.pallas import tpu as pltpu
from jax.sharding import PartitionSpec as P

ITERS = 8
RAMP_WEIGHT = 0.5
PENALTY = 1.0
STEP_PRIMAL = 0.3
STEP_INVEST = 0.5
STEP_DUAL = 0.3
STEP_CAP = 0.05

F32 = jnp.float32
BF16 = jnp.bfloat16
COL_TILE = 256
VMEM_LIMIT = 24 * 1024 * 1024

IN_VMEM = pl.BlockSpec(memory_space=pltpu.VMEM)
IN_PLACE = pl.BlockSpec(memory_space=pl.ANY)


def call(body, name, outs, args, arg_specs=None, scratch=(), aliases=None, flops=0):
    bytes_moved = sum(a.size * a.dtype.itemsize for a in args)
    bytes_moved += sum(o.size * o.dtype.itemsize for o in outs)
    return pl.pallas_call(
        body,
        out_shape=tuple(outs),
        in_specs=arg_specs or [IN_VMEM] * len(args),
        out_specs=tuple(IN_VMEM for _ in outs),
        scratch_shapes=list(scratch),
        input_output_aliases=aliases or {},
        compiler_params=pltpu.CompilerParams(vmem_limit_bytes=VMEM_LIMIT),
        cost_estimate=pl.CostEstimate(flops=flops, bytes_accessed=bytes_moved, transcendentals=0),
        name=name,
    )(*args)


def shape(dims, dtype=F32):
    return jax.ShapeDtypeStruct(tuple(dims), dtype)


def tiles(width):
    return [slice(at, at + COL_TILE) for at in range(0, width, COL_TILE)]


def load_body(mine, *refs):
    (cost, cost_in, disp, disp_in, cap, cap_in, dual, dem,
     cost_out, prim_out, cap_out, dual_out, dem_out, up, down, sems) = refs
    core = lax.rem(lax.axis_index("reg"), 2)
    held = pl.ds(core * mine, mine)
    width = cost.shape[2]
    copies = []
    at = 0
    for src, twin, dst in ((cap, cap_in, cap_out), (disp, disp_in, prim_out), (cost, cost_in, cost_out)):
        copies.append(pltpu.make_async_copy(src.at[held], dst.at[:, :, pl.ds(0, width)], sems.at[at]))
        copies.append(pltpu.make_async_copy(twin, dst.at[:, :, pl.ds(width, width)], sems.at[at + 1]))
        at += 2
    for src, dst in ((dual, dual_out), (dem, dem_out)):
        copies.append(pltpu.make_async_copy(src.at[held], dst, sems.at[at]))
        at += 1
    for copy in copies:
        copy.start()
    for copy in copies:
        copy.wait()
    last = prim_out.shape[1] - 1
    for s in range(mine):
        for cols in tiles(2 * width):
            hour_sum = jnp.sum(cap_out[s, :, cols], axis=0, keepdims=True)
            up[pl.ds(s, 1), cols] = hour_sum
            down[pl.ds(s, 1), cols] = hour_sum
            up[pl.ds(mine + s, 1), cols] = prim_out[s, last:last + 1, cols]
            down[pl.ds(mine + s, 1), cols] = prim_out[s, 0:1, cols]


def primal_body(first, last, others, *refs):
    refs = list(refs)
    take = lambda count: [refs.pop(0) for _ in range(count)]
    matrix, cost, prim, cap, dual, up, down = take(7)
    if not first:
        dem, sent, carry = take(3)
        received = take(others)
    if last:
        keep, give = take(2)
    else:
        prim_out = take(1)[0]
    if not first:
        dual_out = take(1)[0]
    if last:
        rows_out = take(1)[0]
    else:
        sent_out, carry_out = take(2)
    ext_low = take(1)[0]
    mine, hours, width = prim.shape
    hour_place = lax.axis_index("hour")
    hour_ends = lax.axis_size("hour") - 1
    has_prev = (hour_place > 0).astype(F32)
    has_next = (hour_place < hour_ends).astype(F32)
    row = lax.broadcasted_iota(jnp.int32, (hours, COL_TILE), 0)
    half = width // 2
    for s in range(mine):
        multipliers = dual[s]
        if not first:
            image = sent[s].astype(F32)
            for other in received:
                image = image + other[s].astype(F32)
            multipliers = jnp.maximum(multipliers + STEP_DUAL * (dem[s] - image), 0.0)
            dual_out[s] = multipliers
        low = multipliers.astype(BF16)
        for cols in tiles(width):
            pulled = jnp.dot(low, matrix[:, cols], preferred_element_type=F32)
            x = prim[s, :, cols]
            before = up[mine + s:mine + s + 1, cols] * has_prev
            after = down[mine + s:mine + s + 1, cols] * has_next
            prev = jnp.where(row == 0, before, pltpu.roll(x, 1, 0))
            follow = jnp.where(row == hours - 1, after, pltpu.roll(x, hours - 1, 0))
            rough = 2.0 * x - prev - follow
            grad = cost[s, :, cols] + RAMP_WEIGHT * rough - pulled + cap[s, :, cols]
            new = jnp.maximum(x - STEP_PRIMAL * grad, 0.0)
            if last:
                if cols.start < half:
                    keep[s, :, cols] = new
                else:
                    give[s, :, cols.start - half:cols.stop - half] = new
            else:
                prim_out[s, :, cols] = new
            ext_low[:, cols] = (2.0 * new - x).astype(BF16)
        total = lax.dot_general(
            ext_low[...], matrix[...], (((1,), (1,)), ((), ())), preferred_element_type=F32
        )
        if not first:
            total = total + carry[s]
        if last:
            rows_out[s] = total
        else:
            low_sum = total.astype(BF16)
            sent_out[s] = low_sum
            carry_out[s] = total - low_sum.astype(F32)


def mean_and_invest(hours_all, parts, invest, const, s):
    sums = [p[s:s + 1, :] for p in parts]
    while len(sums) > 1:
        sums = [a + b for a, b in zip(sums[0::2], sums[1::2])]
    mean = sums[0] / hours_all
    old = invest[s]
    grad = const[s] + PENALTY * old - mean
    new = jnp.maximum(old - STEP_INVEST * grad, 0.0)
    return old, new


def cap_body(hours_all, parts_count, *refs):
    prim, new, cap, invest, const = refs[:5]
    parts = refs[5:5 + parts_count]
    cap_out, invest_out, up, down = refs[5 + parts_count:]
    mine, hours, width = prim.shape
    for s in range(mine):
        old_inv, new_inv = mean_and_invest(hours_all, parts, invest, const, s)
        invest_out[s] = new_inv
        limit = jnp.sum(2.0 * new_inv - old_inv, axis=0, keepdims=True)
        for cols in tiles(width):
            fresh = new[s, :, cols]
            ext = 2.0 * fresh - prim[s, :, cols]
            c = jnp.maximum(cap[s, :, cols] + STEP_CAP * (ext - limit[:, cols]), 0.0)
            cap_out[s, :, cols] = c
            hour_sum = jnp.sum(c, axis=0, keepdims=True)
            up[pl.ds(s, 1), cols] = hour_sum
            down[pl.ds(s, 1), cols] = hour_sum
            up[pl.ds(mine + s, 1), cols] = fresh[hours - 1:hours]
            down[pl.ds(mine + s, 1), cols] = fresh[0:1]


def invest_body(hours_all, parts_count, *refs):
    invest, const = refs[:2]
    parts = refs[2:2 + parts_count]
    out = refs[2 + parts_count]
    for s in range(invest.shape[0]):
        out[s] = mean_and_invest(hours_all, parts, invest, const, s)[1]


def rotate(x, axis, by):
    count = lax.axis_size(axis)
    return lax.ppermute(x, axis, [(i, (i + by) % count) for i in range(count)])


def hour_exchange(up, down, mine):
    count = lax.axis_size("hour")
    from_prev = rotate(up, "hour", 1)
    from_next = rotate(down, "hour", count - 1)
    own = up[:mine]
    if count == 4:
        far = rotate(own, "hour", 2)
        return from_prev, from_next, (up, far, from_prev, from_next)
    return from_prev, from_next, (lax.psum(own, "hour"),)


def shards(
    cost_rate,
    invest_cost,
    tile,
    tile_mask,
    demand,
    dispatch,
    dual,
    cap_dual,
    capacity,
    multiplier,
    consensus,
    scen_weight,
    node_of,
):
    reg_count = lax.axis_size("reg")
    chips = reg_count // 2
    place = lax.axis_index("reg")
    core = place % 2
    chip = place // 2
    nscen, hours, width = dispatch.shape
    rows = dual.shape[2]
    mine = nscen // 2
    hours_all = float(hours * lax.axis_size("hour"))
    twin = [(i, i ^ 1) for i in range(reg_count)]

    def swap(x):
        return lax.ppermute(x, "reg", twin)

    def held(x):
        return lax.dynamic_slice_in_dim(x, core * mine, mine, 0)

    def given(x):
        return lax.dynamic_slice_in_dim(x, (1 - core) * mine, mine, 0)

    def join(kept, got):
        first = jnp.where(core == 0, kept, got)
        second = jnp.where(core == 0, got, kept)
        return jnp.concatenate([first, second], axis=0)

    cap_in = swap(given(cap_dual))
    disp_in = swap(given(dispatch))
    cost_in = swap(given(cost_rate))
    matrix_own = tile[0] * tile_mask[0].astype(BF16)
    matrix = jnp.concatenate([matrix_own, swap(matrix_own)], axis=1)
    small = jnp.concatenate([invest_cost[None] + multiplier - PENALTY * consensus, capacity], axis=1)
    small_all = jnp.concatenate([held(small), swap(given(small))], axis=2)
    sections = capacity.shape[1]
    const, invest = small_all[:, :sections], small_all[:, sections:]

    full = shape((mine, hours, 2 * width))
    dual_like = shape((mine, hours, rows))
    message = shape((2 * mine, 2 * width))
    cost, prim, cap, dual_var, dem, up, down = call(
        functools.partial(load_body, mine),
        "load",
        (full, full, full, dual_like, dual_like, message, message),
        (cost_rate, cost_in, dispatch, disp_in, cap_dual, cap_in, dual, demand),
        arg_specs=[IN_PLACE] * 8,
        scratch=(pltpu.SemaphoreType.DMA((8,)),),
    )
    flops = 4 * mine * hours * rows * 2 * width
    sent = carry = None
    received = ()
    for step in range(ITERS):
        first, last = step == 0, step + 1 == ITERS
        from_prev, from_next, parts = hour_exchange(up, down, mine)
        args = [matrix, cost, prim, cap, dual_var, from_prev, from_next]
        outs = [shape((mine, hours, width))] * 2 if last else [full]
        aliases = {}
        if not first:
            args += [dem, sent, carry, *received]
            aliases[4] = len(outs)
            outs += [dual_like]
        if last:
            outs += [dual_like]
        else:
            if not first:
                aliases[9] = len(outs) + 1
            outs += [shape(dual_like.shape, BF16), dual_like]
        got = list(
            call(
                functools.partial(primal_body, first, last, chips - 1),
                f"primal_{step}",
                outs,
                args,
                scratch=(pltpu.VMEM((hours, 2 * width), BF16),),
                aliases=aliases,
                flops=flops,
            )
        )
        if last:
            keep, give = got.pop(0), got.pop(0)
        else:
            fresh = got.pop(0)
        if not first:
            dual_var = got.pop(0)
        if last:
            row_sums = got.pop(0)
            (invest,) = call(
                functools.partial(invest_body, hours_all, len(parts)),
                "invest_last",
                (shape(invest.shape),),
                (invest, const, *parts),
            )
        else:
            sent, carry = got
            received = [rotate(sent, "reg", 2 * d) for d in range(1, chips)]
            cap, invest, up, down = call(
                functools.partial(cap_body, hours_all, len(parts)),
                f"cap_{step}",
                (full, shape(invest.shape), message, message),
                (prim, fresh, cap, invest, const, *parts),
                aliases={2: 0, 3: 1},
            )
            prim = fresh

    dispatch_out = join(keep, swap(give))

    chip_rows = rows // chips

    def rows_of(x, c):
        return lax.dynamic_slice_in_dim(x, (c % chips) * chip_rows, chip_rows, 2)

    image = rows_of(row_sums, chip)
    for d in range(1, chips):
        image = image + rotate(rows_of(row_sums, chip + d), "reg", 2 * d)
    dual_last = jnp.maximum(
        rows_of(dual_var, chip) + STEP_DUAL * (rows_of(dem, chip) - image), 0.0
    )
    own_rows = chip_rows // 2
    dual_keep = lax.dynamic_slice_in_dim(dual_last, core * own_rows, own_rows, 2)
    dual_give = lax.dynamic_slice_in_dim(dual_last, (1 - core) * own_rows, own_rows, 2)
    dual_out = join(dual_keep, swap(dual_give))

    capacity_out = join(invest[:, :, :width], swap(invest[:, :, width:]))

    scen_count = lax.axis_size("scen")
    node_count = node_of.shape[1] * scen_count // 2
    node_ids = jnp.arange(node_count, dtype=jnp.int32)
    one_hot = (node_of[:, :, None] == node_ids[None, None, :]).astype(F32)
    weights = one_hot * scen_weight[None, :, None]
    node_sum = jnp.sum(
        weights[:, :, :, None] * jnp.transpose(capacity_out, (1, 0, 2))[:, :, None, :], axis=1
    )
    node_mass = jnp.sum(weights, axis=1)
    packed = jnp.concatenate(
        [node_sum, jnp.broadcast_to(node_mass[:, :, None], node_mass.shape + (128,))], axis=2
    )
    if scen_count == 2:
        packed = packed + rotate(packed, "scen", 1)
    else:
        packed = lax.psum(packed, "scen")
    sum_total, mass_total = packed[:, :, :width], packed[:, :, width:width + 1]
    average = sum_total / (mass_total + (mass_total <= 0.0).astype(F32))
    spread_back = jnp.sum(one_hot[:, :, :, None] * average[:, None, :, :], axis=2)
    multiplier_out = multiplier + PENALTY * (capacity_out - jnp.transpose(spread_back, (1, 0, 2)))
    return (dispatch_out, dual_out, capacity_out, multiplier_out)


def solution(mesh):
    placed = (
        P("scen", "hour", "reg"),
        P(None, "reg"),
        P("hour", None, "reg"),
        P("hour", None, "reg"),
        P("scen", "hour", None),
        P("scen", "hour", "reg"),
        P("scen", "hour", None),
        P("scen", "hour", "reg"),
        P("scen", None, "reg"),
        P("scen", None, "reg"),
        P("scen", None, "reg"),
        P("scen"),
        P(None, "scen"),
    )
    return jax.shard_map(
        shards,
        mesh=mesh,
        in_specs=placed,
        out_specs=(
            P("scen", "hour", "reg"),
            P("scen", "hour", "reg"),
            P("scen", None, "reg"),
            P("scen", None, "reg"),
        ),
        check_vma=False,
    )
```

```python
import functools
import math

import jax
import jax.numpy as jnp
from jax import lax
from jax.experimental import pallas as pl
from jax.experimental.pallas import tpu as pltpu
from jax.sharding import PartitionSpec as P

ITERS = 8
RAMP_WEIGHT = 0.5
PENALTY = 1.0
STEP_PRIMAL = 0.3
STEP_INVEST = 0.5
STEP_DUAL = 0.3
STEP_CAP = 0.05

F32 = jnp.float32
BF16 = jnp.bfloat16
COL_TILE = 256
VMEM_LIMIT = 24 * 1024 * 1024

IN_VMEM = pl.BlockSpec(memory_space=pltpu.VMEM)
IN_HBM = pl.BlockSpec(memory_space=pltpu.HBM)


def call(body, outs, args, arg_specs=None, out_specs=None, scratch=(), aliases=None, flops=0):
    if arg_specs is not None:
        args = [
            pltpu.with_memory_space_constraint(a, pltpu.HBM) if spec is IN_HBM else a
            for a, spec in zip(args, arg_specs)
        ]
    bytes_moved = sum(a.size * a.dtype.itemsize for a in args)
    bytes_moved += sum(math.prod(o.shape) * jnp.dtype(o.dtype).itemsize for o in outs)
    return pl.pallas_call(
        body,
        out_shape=tuple(outs),
        in_specs=arg_specs or [IN_VMEM] * len(args),
        out_specs=out_specs or tuple(IN_VMEM for _ in outs),
        scratch_shapes=list(scratch),
        input_output_aliases=aliases or {},
        compiler_params=pltpu.CompilerParams(vmem_limit_bytes=VMEM_LIMIT),
        cost_estimate=pl.CostEstimate(flops=flops, bytes_accessed=bytes_moved, transcendentals=0),
    )(*args)


def shape(dims, dtype=F32):
    return jax.ShapeDtypeStruct(tuple(dims), dtype)


def in_vmem(dims, dtype=F32):
    return pltpu.VMEM(tuple(dims), dtype)


def tiles(width):
    return [
        (half, slice(at, at + COL_TILE), slice(half * width + at, half * width + at + COL_TILE))
        for half in range(2)
        for at in range(0, width, COL_TILE)
    ]


def run_copies(pairs, sems):
    copies = [pltpu.make_async_copy(a, b, sems.at[i]) for i, (a, b) in enumerate(pairs)]
    for copy in copies:
        copy.start()
    for copy in copies:
        copy.wait()


def give_body(mine, *refs):
    count = (len(refs) - 1) // 2
    core = lax.rem(lax.axis_index("reg"), 2)
    given = pl.ds((1 - core) * mine, mine)
    run_copies([(refs[i].at[given], refs[count + i]) for i in range(count)], refs[-1])


def held_body(mine, *refs):
    count = (len(refs) - 1) // 2
    core = lax.rem(lax.axis_index("reg"), 2)
    held = pl.ds(core * mine, mine)
    run_copies([(refs[i].at[held], refs[count + i]) for i in range(count)], refs[-1])


def matrix_body(tile, mask, out):
    out[...] = tile[0] * mask[0].astype(F32).astype(BF16)


def message_body(paired, *refs):
    cap, prim, parts = refs[:2], refs[2:4], refs[4:6]
    matrix, near, far = refs[6:]
    mine, _, width = cap[0].shape
    for half in range(2):
        matrix[:, half * width:(half + 1) * width] = parts[half][...]
    for s in range(mine):
        for half, cols, flat in tiles(width):
            write_message(paired, near, far, s, flat, cap[half][s, :, cols], prim[half][s, :, cols])


def is_odd():
    return lax.rem(lax.axis_index("hour"), 2) == 1


def write_message(paired, near, far, s, flat, c, x):
    mine = near.shape[0] // 2
    hours = x.shape[0]
    hour_sum = jnp.sum(c, axis=0, keepdims=True)
    near[pl.ds(s, 1), flat] = hour_sum
    far[pl.ds(s, 1), flat] = hour_sum
    first, last = x[0:1], x[hours - 1:hours]
    if paired:
        odd = is_odd()
        first, last = jnp.where(odd, last, first), jnp.where(odd, first, last)
    near[pl.ds(mine + s, 1), flat] = last
    far[pl.ds(mine + s, 1), flat] = first


def step_body(hours_all, paired, sums_count, first, last, *refs):
    refs = list(refs)
    take = lambda count: [refs.pop(0) for _ in range(count)]
    matrix, cost, prim, cap = take(1)[0], take(2), take(2), take(2)
    dual, invest, const, near, far = take(5)
    sums = take(sums_count)
    if not first:
        dem, sent, carry, received = take(4)
    prim_out = take(2)
    if last:
        inv_keep, inv_give, base_out, rows_give = take(4)
    else:
        cap_out = take(2)
        invest_out, near_out, far_out, sent_out, carry_out = take(5)
        if not first:
            dual_out = take(1)[0]
    ext_low = take(1)[0]
    mine, hours, width = prim[0].shape
    chip = lax.axis_index("reg") // 2
    place = lax.axis_index("hour")
    has_prev = (place > 0).astype(F32)
    has_next = (place < lax.axis_size("hour") - 1).astype(F32)
    row = lax.broadcasted_iota(jnp.int32, (hours, COL_TILE), 0)
    for s in range(mine):
        multipliers = dual[s]
        if not first:
            image = sent[s].astype(F32) + received[s].astype(F32)
            multipliers = jnp.maximum(multipliers + STEP_DUAL * (dem[s] - image), 0.0)
            if not last:
                dual_out[s] = multipliers
        low = multipliers.astype(BF16)
        parts = [part[s:s + 1, :] for part in sums]
        while len(parts) > 1:
            parts = [u + v for u, v in zip(parts[0::2], parts[1::2])]
        old_inv = invest[s]
        grad_inv = const[s] + PENALTY * old_inv - parts[0] / hours_all
        new_inv = jnp.maximum(old_inv - STEP_INVEST * grad_inv, 0.0)
        if last:
            inv_keep[s] = new_inv[:, :width]
            inv_give[s] = new_inv[:, width:]
        else:
            invest_out[s] = new_inv
        limit = jnp.sum(2.0 * new_inv - old_inv, axis=0, keepdims=True)
        before = near[mine + s:mine + s + 1, :]
        after = far[mine + s:mine + s + 1, :]
        if paired:
            odd = is_odd()
            before, after = jnp.where(odd, before, after), jnp.where(odd, after, before)
        before = before * has_prev
        after = after * has_next
        for half, cols, flat in tiles(width):
            pulled = jnp.dot(low, matrix[:, flat], preferred_element_type=F32)
            x = prim[half][s, :, cols]
            prev = jnp.where(row == 0, before[:, flat], pltpu.roll(x, 1, 0))
            follow = jnp.where(row == hours - 1, after[:, flat], pltpu.roll(x, hours - 1, 0))
            rough = 2.0 * x - prev - follow
            c = cap[half][s, :, cols]
            grad = cost[half][s, :, cols] + RAMP_WEIGHT * rough - pulled + c
            new = jnp.maximum(x - STEP_PRIMAL * grad, 0.0)
            prim_out[half][s, :, cols] = new
            ext = 2.0 * new - x
            ext_low[:, flat] = ext.astype(BF16)
            if not last:
                c = jnp.maximum(c + STEP_CAP * (ext - limit[:, flat]), 0.0)
                cap_out[half][s, :, cols] = c
                write_message(paired, near_out, far_out, s, flat, c, new)
        total = lax.dot_general(
            ext_low[...], matrix[...], (((1,), (1,)), ((), ())), preferred_element_type=F32
        )
        if not first:
            total = total + carry[s]
        if last:
            rows = total.shape[1] // 2
            low_chip = chip == 0
            keep = jnp.where(low_chip, total[:, :rows], total[:, rows:])
            rows_give[s] = jnp.where(low_chip, total[:, rows:], total[:, :rows])
            base = multipliers + STEP_DUAL * dem[s]
            base_out[s] = jnp.where(low_chip, base[:, :rows], base[:, rows:]) - STEP_DUAL * keep
        else:
            low_sum = total.astype(BF16)
            sent_out[s] = low_sum
            carry_out[s] = total - low_sum.astype(F32)


def join_body(*refs):
    kept, got, out, sems = refs
    mine = kept.shape[0]
    core = lax.rem(lax.axis_index("reg"), 2)
    run_copies(
        [(kept, out.at[pl.ds(core * mine, mine)]), (got, out.at[pl.ds((1 - core) * mine, mine)])],
        sems,
    )


def join(kept, got):
    mine = kept.shape[0]
    return call(
        join_body,
        (shape((2 * mine,) + kept.shape[1:]),),
        (kept, got),
        out_specs=(IN_HBM,),
        scratch=(pltpu.SemaphoreType.DMA((2,)),),
    )[0]


def dual_body(base, got, keep, give):
    core = lax.rem(lax.axis_index("reg"), 2)
    part = keep.shape[2]
    for s in range(base.shape[0]):
        new = jnp.maximum(base[s] - STEP_DUAL * got[s], 0.0)
        low, high = new[:, :part], new[:, part:]
        keep[s] = jnp.where(core == 0, low, high)
        give[s] = jnp.where(core == 0, high, low)


def hour_exchange(near, far, mine, paired):
    count = lax.axis_size("hour")
    if not paired:
        near_in = lax.ppermute(near, "hour", [(i, (i + 1) % count) for i in range(count)])
        far_in = lax.ppermute(far, "hour", [((i + 1) % count, i) for i in range(count)])
        return near_in, far_in, (lax.psum(near[:mine], "hour"),)
    partners = lambda by: [(i, i ^ by) for i in range(count)]
    far_in = lax.ppermute(far, "hour", partners(3))
    near_in = lax.ppermute(near, "hour", partners(1))
    across = lax.ppermute(near[:mine], "hour", partners(2))
    return near_in, far_in, (near, near_in, across, far_in)


def shards(
    cost_rate,
    invest_cost,
    tile,
    tile_mask,
    demand,
    dispatch,
    dual,
    cap_dual,
    capacity,
    multiplier,
    consensus,
    scen_weight,
    node_of,
):
    reg_count = lax.axis_size("reg")
    assert reg_count == 4
    paired = lax.axis_size("hour") == 4
    core = lax.axis_index("reg") % 2
    nscen, hours, width = dispatch.shape
    rows = dual.shape[2]
    mine = nscen // 2
    sections = capacity.shape[1]
    hours_all = float(hours * lax.axis_size("hour"))
    twin = [(i, i ^ 1) for i in range(reg_count)]
    other_chip = [(i, i ^ 2) for i in range(reg_count)]
    half_full = in_vmem((mine, hours, width))
    dual_like = in_vmem((mine, hours, rows))
    message = in_vmem((2 * mine, 2 * width))
    invest_like = in_vmem((mine, sections, 2 * width))

    def held(x):
        return lax.dynamic_slice_in_dim(x, core * mine, mine, 0)

    def given(x):
        return lax.dynamic_slice_in_dim(x, (1 - core) * mine, mine, 0)

    prim_give, cap_give, cost_give = call(
        functools.partial(give_body, mine),
        (half_full,) * 3,
        (dispatch, cap_dual, cost_rate),
        arg_specs=[IN_HBM] * 3,
        scratch=(pltpu.SemaphoreType.DMA((3,)),),
    )
    prim_twin = lax.ppermute(prim_give, "reg", twin)
    cap_twin = lax.ppermute(cap_give, "reg", twin)
    cost_twin = lax.ppermute(cost_give, "reg", twin)
    (matrix_own,) = call(matrix_body, (in_vmem(tile.shape[1:], BF16),), (tile, tile_mask))
    matrix_twin = lax.ppermute(matrix_own, "reg", twin)
    prim_own, cap_own, cost_own, dual_var, dem = call(
        functools.partial(held_body, mine),
        (half_full,) * 3 + (dual_like,) * 2,
        (dispatch, cap_dual, cost_rate, dual, demand),
        arg_specs=[IN_HBM] * 5,
        scratch=(pltpu.SemaphoreType.DMA((5,)),),
    )
    prim, cap, cost = (prim_own, prim_twin), (cap_own, cap_twin), (cost_own, cost_twin)
    matrix, near, far = call(
        functools.partial(message_body, paired),
        (in_vmem((rows, 2 * width), BF16), message, message),
        (*cap, *prim, matrix_own, matrix_twin),
    )
    small = jnp.concatenate(
        [invest_cost[None] + multiplier - PENALTY * consensus, capacity], axis=1
    )
    small_all = jnp.concatenate([held(small), lax.ppermute(given(small), "reg", twin)], axis=2)
    const, invest = small_all[:, :sections], small_all[:, sections:]

    flops = 4 * mine * hours * rows * 2 * width
    sent = carry = received = None
    for step in range(ITERS):
        first, last = step == 0, step + 1 == ITERS
        near_in, far_in, sums = hour_exchange(near, far, mine, paired)
        args = [matrix, *cost, *prim, *cap, dual_var, invest, const, near_in, far_in, *sums]
        if not first:
            args += [dem, sent, carry, received]
        if last:
            outs = [half_full] * 2 + [in_vmem((mine, sections, width))] * 2
            outs += [in_vmem((mine, hours, rows // 2))] * 2
        else:
            outs = [half_full] * 4 + [invest_like, message, message]
            outs += [in_vmem((mine, hours, rows), BF16), dual_like]
            if not first:
                outs += [dual_like]
        got = call(
            functools.partial(step_body, hours_all, paired, len(sums), first, last),
            outs,
            args,
            scratch=(pltpu.VMEM((hours, 2 * width), BF16),),
            flops=flops,
        )
        prim = got[:2]
        if last:
            inv_keep, inv_give, base, rows_give = got[2:]
        else:
            cap = got[2:4]
            invest, near, far, sent, carry = got[4:9]
            received = lax.ppermute(sent, "reg", other_chip)
            if not first:
                dual_var = got[9]

    rows_got = lax.ppermute(rows_give, "reg", other_chip)
    prim_got = lax.ppermute(prim[1], "reg", twin)
    inv_got = lax.ppermute(inv_give, "reg", twin)
    capacity_out = jnp.where(
        core == 0,
        jnp.concatenate([inv_keep, inv_got], axis=0),
        jnp.concatenate([inv_got, inv_keep], axis=0),
    )
    scen_count = lax.axis_size("scen")
    node_count = node_of.shape[1] * scen_count // 2
    node_ids = jnp.arange(node_count, dtype=jnp.int32)
    one_hot = (node_of[:, :, None] == node_ids[None, None, :]).astype(F32)
    weights = one_hot * scen_weight[None, :, None]
    node_sum = jnp.sum(
        weights[:, :, :, None] * jnp.transpose(capacity_out, (1, 0, 2))[:, :, None, :], axis=1
    )
    node_mass = jnp.sum(weights, axis=1)
    packed = jnp.concatenate(
        [node_sum, jnp.broadcast_to(node_mass[:, :, None], node_mass.shape + (128,))], axis=2
    )
    if scen_count == 2:
        packed = packed + lax.ppermute(packed, "scen", [(0, 1), (1, 0)])
    else:
        packed = lax.psum(packed, "scen")
    sum_total, mass_total = packed[:, :, :width], packed[:, :, width:width + 1]
    average = sum_total / (mass_total + (mass_total <= 0.0).astype(F32))
    spread_back = jnp.sum(one_hot[:, :, :, None] * average[:, None, :, :], axis=2)
    multiplier_out = multiplier + PENALTY * (capacity_out - jnp.transpose(spread_back, (1, 0, 2)))

    dispatch_out = join(prim[0], prim_got)
    dual_keep, dual_give = call(
        dual_body, (in_vmem((mine, hours, rows // reg_count)),) * 2, (base, rows_got)
    )
    dual_got = lax.ppermute(dual_give, "reg", twin)
    dual_out = jnp.where(
        core == 0,
        jnp.concatenate([dual_keep, dual_got], axis=0),
        jnp.concatenate([dual_got, dual_keep], axis=0),
    )
    return (dispatch_out, dual_out, capacity_out, multiplier_out)


def solution(mesh):
    placed = (
        P("scen", "hour", "reg"),
        P(None, "reg"),
        P("hour", None, "reg"),
        P("hour", None, "reg"),
        P("scen", "hour", None),
        P("scen", "hour", "reg"),
        P("scen", "hour", None),
        P("scen", "hour", "reg"),
        P("scen", None, "reg"),
        P("scen", None, "reg"),
        P("scen", None, "reg"),
        P("scen"),
        P(None, "scen"),
    )
    return jax.shard_map(
        shards,
        mesh=mesh,
        in_specs=placed,
        out_specs=(
            P("scen", "hour", "reg"),
            P("scen", "hour", "reg"),
            P("scen", None, "reg"),
            P("scen", None, "reg"),
        ),
        check_vma=False,
    )
```

```python
import functools
import math

import jax
import jax.numpy as jnp
from jax import lax
from jax.experimental import pallas as pl
from jax.experimental.pallas import tpu as pltpu
from jax.sharding import PartitionSpec as P


ITERS = 8
RAMP_WEIGHT = 0.5
PENALTY = 1.0
STEP_PRIMAL = 0.3
STEP_INVEST = 0.5
STEP_DUAL = 0.3
STEP_CAP = 0.05

F32 = jnp.float32
BF16 = jnp.bfloat16
COL_TILE = 256
VMEM_LIMIT = 24 * 1024 * 1024

IN_VMEM = pl.BlockSpec(memory_space=pltpu.VMEM)
IN_SMEM = pl.BlockSpec(memory_space=pltpu.SMEM)
IN_HBM = pl.BlockSpec(memory_space=pltpu.HBM)


def call(body, outs, args, arg_specs=None, out_specs=None, scratch=(), aliases=None, flops=0):
    if arg_specs is not None:
        args = [
            pltpu.with_memory_space_constraint(a, pltpu.HBM) if spec is IN_HBM else a
            for a, spec in zip(args, arg_specs)
        ]
    bytes_moved = sum(a.size * a.dtype.itemsize for a in args)
    bytes_moved += sum(math.prod(o.shape) * jnp.dtype(o.dtype).itemsize for o in outs)
    return pl.pallas_call(
        body,
        out_shape=tuple(outs),
        in_specs=arg_specs or [IN_VMEM] * len(args),
        out_specs=out_specs or tuple(IN_VMEM for _ in outs),
        scratch_shapes=list(scratch),
        input_output_aliases=aliases or {},
        compiler_params=pltpu.CompilerParams(vmem_limit_bytes=VMEM_LIMIT),
        cost_estimate=pl.CostEstimate(flops=flops, bytes_accessed=bytes_moved, transcendentals=0),
    )(*args)


def shape(dims, dtype=F32):
    return jax.ShapeDtypeStruct(tuple(dims), dtype)


def in_vmem(dims, dtype=F32):
    return pltpu.VMEM(tuple(dims), dtype)


def tiles(width):
    return [
        (half, slice(at, at + COL_TILE), slice(half * width + at, half * width + at + COL_TILE))
        for half in range(2)
        for at in range(0, width, COL_TILE)
    ]


def run_copies(pairs, sems):
    copies = [pltpu.make_async_copy(a, b, sems.at[i]) for i, (a, b) in enumerate(pairs)]
    for copy in copies:
        copy.start()
    for copy in copies:
        copy.wait()


def give_body(mine, *refs):
    *sources, out, sems = refs
    core = lax.rem(lax.axis_index("reg"), 2)
    given = pl.ds((1 - core) * mine, mine)
    run_copies([(src.at[given], out.at[i]) for i, src in enumerate(sources)], sems)


def held_body(mine, *refs):
    *sources, out, dual_out, dem_out, sems = refs
    core = lax.rem(lax.axis_index("reg"), 2)
    held = pl.ds(core * mine, mine)
    targets = [out.at[0], out.at[1], out.at[2], dual_out, dem_out]
    run_copies([(src.at[held], dst) for src, dst in zip(sources, targets)], sems)


def small_body(cost, mult, cons, capacity, own, give):
    sections = cost.shape[0]
    mine = own.shape[1]
    core = lax.rem(lax.axis_index("reg"), 2)
    for g in range(sections):
        const = cost[g:g + 1, :] + mult[g] - PENALTY * cons[g]
        for at, x in ((g, const), (sections + g, capacity[g])):
            own[at] = jnp.where(core == 0, x[:mine], x[mine:])
            give[at] = jnp.where(core == 0, x[mine:], x[:mine])


def matrix_body(tile, mask, out):
    out[...] = tile[0] * mask[0].astype(F32).astype(BF16)


def message_body(paired, own, twin, part, part_in, small, small_in, *outs):
    matrix, const, invest, near, far = outs
    _, mine, _, width = own.shape
    sections = invest.shape[0]
    matrix[:, :width] = part[...]
    matrix[:, width:] = part_in[...]
    for src, cols in ((small, slice(0, width)), (small_in, slice(width, 2 * width))):
        const[:, :, cols] = src[:sections]
        invest[:, :, cols] = src[sections:]
    both = (own, twin)
    for s in range(mine):
        for half, cols, flat in tiles(width):
            src = both[half]
            write_message(paired, near, far, s, flat, src[1, s, :, cols], src[0, s, :, cols])


def is_odd():
    return lax.rem(lax.axis_index("hour"), 2) == 1


def write_message(paired, near, far, s, flat, c, x):
    mine = near.shape[0] // 2
    hours = x.shape[0]
    hour_sum = jnp.sum(c, axis=0, keepdims=True)
    near[pl.ds(s, 1), flat] = hour_sum
    far[pl.ds(s, 1), flat] = hour_sum
    first, last = x[0:1], x[hours - 1:hours]
    if paired:
        odd = is_odd()
        first, last = jnp.where(odd, last, first), jnp.where(odd, first, last)
    near[pl.ds(mine + s, 1), flat] = last
    far[pl.ds(mine + s, 1), flat] = first


def new_invest(hours_all, sums, invest, const):
    mine = invest.shape[1]
    parts = [part[:mine, :] for part in sums]
    while len(parts) > 1:
        parts = [u + v for u, v in zip(parts[0::2], parts[1::2])]
    mean = parts[0] / hours_all
    olds = [invest[g] for g in range(invest.shape[0])]
    news = [
        jnp.maximum(old - STEP_INVEST * (const[g] + PENALTY * old - mean), 0.0)
        for g, old in enumerate(olds)
    ]
    return olds, news


def invest_body(hours_all, sums_count, *refs):
    invest, const = refs[:2]
    keep, give = refs[2 + sums_count:]
    width = keep.shape[2]
    for g, new in enumerate(new_invest(hours_all, refs[2:2 + sums_count], invest, const)[1]):
        keep[g] = new[:, :width]
        give[g] = new[:, width:]


def step_body(hours_all, paired, sums_count, first, last, *refs):
    refs = list(refs)
    take = lambda count: [refs.pop(0) for _ in range(count)]
    matrix, own, twin, dual, near, far = take(6)
    both = (own, twin)
    cost = [src.at[2] for src in both]
    if first:
        prim, cap = [src.at[0] for src in both], [src.at[1] for src in both]
    else:
        prim, cap = take(2), take(2)
        dem, sent, carry, received = take(4)
    if not last:
        invest, const = take(2)
        sums = take(sums_count)
    prim_out = take(2)
    if last:
        base_out, rows_give = take(2)
    else:
        cap_out = take(2)
        invest_out, near_out, far_out, sent_out, carry_out = take(5)
        if not first:
            dual_out = take(1)[0]
        olds, news = new_invest(hours_all, sums, invest, const)
        limits = 0.0
        for g, (old, new) in enumerate(zip(olds, news)):
            invest_out[g] = new
            limits = limits + (2.0 * new - old)
    ext_low = take(1)[0]
    mine, hours, width = prim[0].shape
    chip = lax.axis_index("reg") // 2
    place = lax.axis_index("hour")
    has_prev = (place > 0).astype(F32)
    has_next = (place < lax.axis_size("hour") - 1).astype(F32)
    row = lax.broadcasted_iota(jnp.int32, (hours, COL_TILE), 0)
    for s in range(mine):
        multipliers = dual[s]
        if not first:
            image = sent[s].astype(F32) + received[s].astype(F32)
            multipliers = jnp.maximum(multipliers + STEP_DUAL * (dem[s] - image), 0.0)
            if not last:
                dual_out[s] = multipliers
        low = multipliers.astype(BF16)
        if not last:
            limit = limits[s:s + 1, :]
        before = near[mine + s:mine + s + 1, :]
        after = far[mine + s:mine + s + 1, :]
        if paired:
            odd = is_odd()
            before, after = jnp.where(odd, before, after), jnp.where(odd, after, before)
        before = before * has_prev
        after = after * has_next
        for half, cols, flat in tiles(width):
            pulled = jnp.dot(low, matrix[:, flat], preferred_element_type=F32)
            x = prim[half][s, :, cols]
            prev = jnp.where(row == 0, before[:, flat], pltpu.roll(x, 1, 0))
            follow = jnp.where(row == hours - 1, after[:, flat], pltpu.roll(x, hours - 1, 0))
            rough = 2.0 * x - prev - follow
            c = cap[half][s, :, cols]
            grad = cost[half][s, :, cols] + RAMP_WEIGHT * rough - pulled + c
            new = jnp.maximum(x - STEP_PRIMAL * grad, 0.0)
            prim_out[half][s, :, cols] = new
            ext = 2.0 * new - x
            ext_low[:, flat] = ext.astype(BF16)
            if not last:
                c = jnp.maximum(c + STEP_CAP * (ext - limit[:, flat]), 0.0)
                cap_out[half][s, :, cols] = c
                write_message(paired, near_out, far_out, s, flat, c, new)
        total = lax.dot_general(
            ext_low[...], matrix[...], (((1,), (1,)), ((), ())), preferred_element_type=F32
        )
        if not first:
            total = total + carry[s]
        if last:
            rows = total.shape[1] // 2
            low_chip = chip == 0
            keep = jnp.where(low_chip, total[:, :rows], total[:, rows:])
            rows_give[s] = jnp.where(low_chip, total[:, rows:], total[:, :rows])
            base = multipliers + STEP_DUAL * dem[s]
            base_out[s] = jnp.where(low_chip, base[:, :rows], base[:, rows:]) - STEP_DUAL * keep
        else:
            low_sum = total.astype(BF16)
            sent_out[s] = low_sum
            carry_out[s] = total - low_sum.astype(F32)


def join_body(*refs):
    kept, got, out, sems = refs
    mine = kept.shape[0]
    core = lax.rem(lax.axis_index("reg"), 2)
    run_copies(
        [(kept, out.at[pl.ds(core * mine, mine)]), (got, out.at[pl.ds((1 - core) * mine, mine)])],
        sems,
    )


def join(kept, got):
    mine = kept.shape[0]
    return call(
        join_body,
        (shape((2 * mine,) + kept.shape[1:]),),
        (kept, got),
        out_specs=(IN_HBM,),
        scratch=(pltpu.SemaphoreType.DMA((2,)),),
    )[0]


def dual_body(base, got, out, give, kept, sem):
    core = lax.rem(lax.axis_index("reg"), 2)
    mine, part = give.shape[:2]
    for s in range(mine):
        new = jnp.maximum(base[s] - STEP_DUAL * got[s], 0.0).T
        low, high = new[:part], new[part:]
        kept[s] = jnp.where(core == 0, low, high)
        give[s] = jnp.where(core == 0, high, low)
    run_copies([(kept, out.at[pl.ds(core * mine, mine)])], sem)


def rest_body(got, _, out, sem):
    core = lax.rem(lax.axis_index("reg"), 2)
    mine = got.shape[0]
    run_copies([(got, out.at[pl.ds((1 - core) * mine, mine)])], sem)


def node_weights(nodes, weights, g, s, n):
    return jnp.where(nodes[g, s] == n, weights[s], 0.0)


def nodes_body(node_count, keep, got, nodes, weights, capacity, packed):
    core = lax.rem(lax.axis_index("reg"), 2)
    sections, mine, width = keep.shape
    for g in range(sections):
        first = jnp.where(core == 0, keep[g], got[g])
        second = jnp.where(core == 0, got[g], keep[g])
        capacity[g, :mine] = first
        capacity[g, mine:] = second
        for n in range(node_count):
            total = jnp.zeros((1, width), F32)
            mass = jnp.zeros((1, 128), F32)
            for s in range(2 * mine):
                weight = node_weights(nodes, weights, g, s, n)
                row = first[s:s + 1] if s < mine else second[s - mine:s - mine + 1]
                total = total + weight * row
                mass = mass + weight
            packed[g, n:n + 1, :width] = total
            packed[g, n:n + 1, width:] = mass


def multiplier_body(mult, capacity, nodes, *refs):
    *packs, out = refs
    sections, scens, width = capacity.shape
    for g in range(sections):
        packed = packs[0][g]
        for other in packs[1:]:
            packed = packed + other[g]
        mass = packed[:, width:width + 1]
        average = packed[:, :width] / jnp.where(mass > 0.0, mass, 1.0)
        for s in range(scens):
            mine = jnp.zeros((1, width), F32)
            for n in range(packed.shape[0]):
                mine = mine + jnp.where(nodes[g, s] == n, average[n:n + 1], 0.0)
            out[g, s:s + 1] = mult[g, s:s + 1] + PENALTY * (capacity[g, s:s + 1] - mine)


def hour_exchange(near, far, mine, paired):
    count = lax.axis_size("hour")
    if not paired:
        near_in = lax.ppermute(near, "hour", [(i, (i + 1) % count) for i in range(count)])
        far_in = lax.ppermute(far, "hour", [((i + 1) % count, i) for i in range(count)])
        return near_in, far_in, (lax.psum(near[:mine], "hour"),)
    partners = lambda by: [(i, i ^ by) for i in range(count)]
    far_in = lax.ppermute(far, "hour", partners(3))
    near_in = lax.ppermute(near, "hour", partners(1))
    across = lax.ppermute(near[:mine], "hour", partners(2))
    return near_in, far_in, (near, near_in, across, far_in)


def shards(
    cost_rate,
    invest_cost,
    tile,
    tile_mask,
    demand,
    dispatch,
    dual,
    cap_dual,
    capacity,
    multiplier,
    consensus,
    scen_weight,
    node_of,
):
    reg_count = lax.axis_size("reg")
    assert reg_count == 4
    paired = lax.axis_size("hour") == 4
    nscen, hours, width = dispatch.shape
    rows = dual.shape[2]
    mine = nscen // 2
    sections = capacity.shape[1]
    hours_all = float(hours * lax.axis_size("hour"))
    twin = [(i, i ^ 1) for i in range(reg_count)]
    other_chip = [(i, i ^ 2) for i in range(reg_count)]
    half_full = in_vmem((mine, hours, width))
    three = in_vmem((3, mine, hours, width))
    dual_like = in_vmem((mine, hours, rows))
    message = in_vmem((2 * mine, 2 * width))
    invest_like = in_vmem((sections, mine, 2 * width))
    small_like = in_vmem((2 * sections, mine, width))
    inv_half = in_vmem((sections, mine, width))
    by_section = lambda x: jnp.transpose(x, (1, 0, 2))
    mult, cons, caps = by_section(multiplier), by_section(consensus), by_section(capacity)

    (give,) = call(
        functools.partial(give_body, mine),
        (three,),
        (dispatch, cap_dual, cost_rate),
        arg_specs=[IN_HBM] * 3,
        scratch=(pltpu.SemaphoreType.DMA((3,)),),
    )
    twin_in = lax.ppermute(give, "reg", twin)
    (part,) = call(matrix_body, (in_vmem(tile.shape[1:], BF16),), (tile, tile_mask))
    part_in = lax.ppermute(part, "reg", twin)
    small, small_give = call(small_body, (small_like,) * 2, (invest_cost, mult, cons, caps))
    small_in = lax.ppermute(small_give, "reg", twin)
    own, dual_var, dem = call(
        functools.partial(held_body, mine),
        (three, dual_like, dual_like),
        (dispatch, cap_dual, cost_rate, dual, demand),
        arg_specs=[IN_HBM] * 5,
        scratch=(pltpu.SemaphoreType.DMA((5,)),),
    )
    matrix, const, invest, near, far = call(
        functools.partial(message_body, paired),
        (in_vmem((rows, 2 * width), BF16), invest_like, invest_like, message, message),
        (own, twin_in, part, part_in, small, small_in),
    )
    near_in, far_in, sums = hour_exchange(near, far, mine, paired)

    flops = 4 * mine * hours * rows * 2 * width
    prim = cap = ()
    sent = carry = received = None
    for step in range(ITERS):
        first, last = step == 0, step + 1 == ITERS
        args = [matrix, own, twin_in, dual_var, near_in, far_in, *prim, *cap]
        if not first:
            args += [dem, sent, carry, received]
        outs = [half_full] * 2
        if last:
            inv_keep, inv_give = call(
                functools.partial(invest_body, hours_all, len(sums)),
                (inv_half,) * 2,
                (invest, const, *sums),
            )
            inv_got = lax.ppermute(inv_give, "reg", twin)
            outs += [in_vmem((mine, hours, rows // 2))] * 2
        else:
            args += [invest, const, *sums]
            outs += [half_full] * 2 + [invest_like, message, message]
            outs += [in_vmem((mine, hours, rows), BF16), dual_like]
            if not first:
                outs += [dual_like]
        got = call(
            functools.partial(step_body, hours_all, paired, len(sums), first, last),
            outs,
            args,
            scratch=(pltpu.VMEM((hours, 2 * width), BF16),),
            flops=flops,
        )
        prim = got[:2]
        if not last:
            cap = got[2:4]
            invest, near, far, sent, carry = got[4:9]
            received = lax.ppermute(sent, "reg", other_chip)
            if not first:
                dual_var = got[9]
            near_in, far_in, sums = hour_exchange(near, far, mine, paired)
            continue
        base, rows_give = got[2:]
        rows_got = lax.ppermute(rows_give, "reg", other_chip)
        prim_got = lax.ppermute(prim[1], "reg", twin)
        scen_count = lax.axis_size("scen")
        node_count = node_of.shape[1] * scen_count // 2
        packed_like = in_vmem((sections, node_count, width + 128))
        by_scen = in_vmem((sections, nscen, width))
        capacity_out, packed = call(
            functools.partial(nodes_body, node_count),
            (by_scen, packed_like),
            (inv_keep, inv_got, node_of, scen_weight),
            arg_specs=[IN_VMEM, IN_VMEM, IN_SMEM, IN_SMEM],
        )
        if scen_count == 2:
            packs = (packed, lax.ppermute(packed, "scen", [(0, 1), (1, 0)]))
        else:
            packs = (lax.psum(packed, "scen"),)
        (multiplier_out,) = call(
            multiplier_body,
            (by_scen,),
            (mult, capacity_out, node_of, *packs),
            arg_specs=[IN_VMEM, IN_VMEM, IN_SMEM] + [IN_VMEM] * len(packs),
        )
        dispatch_out = join(prim[0], prim_got)
        own_rows = rows // reg_count
        dual_half, dual_give = call(
            dual_body,
            (shape((nscen, own_rows, hours)), in_vmem((mine, own_rows, hours))),
            (base, rows_got),
            out_specs=(IN_HBM, IN_VMEM),
            scratch=(pltpu.VMEM((mine, own_rows, hours), F32), pltpu.SemaphoreType.DMA((1,))),
        )
        dual_got = lax.ppermute(dual_give, "reg", twin)
        (dual_out,) = call(
            rest_body,
            (shape(dual_half.shape),),
            (dual_got, dual_half),
            arg_specs=[IN_VMEM, IN_HBM],
            out_specs=(IN_HBM,),
            scratch=(pltpu.SemaphoreType.DMA((1,)),),
            aliases={1: 0},
        )
    return (
        dispatch_out,
        jnp.transpose(dual_out, (0, 2, 1)),
        by_section(capacity_out),
        by_section(multiplier_out),
    )


def solution(mesh):
    placed = (
        P("scen", "hour", "reg"),
        P(None, "reg"),
        P("hour", None, "reg"),
        P("hour", None, "reg"),
        P("scen", "hour", None),
        P("scen", "hour", "reg"),
        P("scen", "hour", None),
        P("scen", "hour", "reg"),
        P("scen", None, "reg"),
        P("scen", None, "reg"),
        P("scen", None, "reg"),
        P("scen"),
        P(None, "scen"),
    )
    return jax.shard_map(
        shards,
        mesh=mesh,
        in_specs=placed,
        out_specs=(
            P("scen", "hour", "reg"),
            P("scen", "hour", "reg"),
            P("scen", None, "reg"),
            P("scen", None, "reg"),
        ),
        check_vma=False,
    )
```

```python
import functools
import math

import jax
import jax.numpy as jnp
from jax import lax
from jax.experimental import pallas as pl
from jax.experimental.pallas import tpu as pltpu
from jax.sharding import PartitionSpec as P


ITERS = 8
RAMP_WEIGHT = 0.5
PENALTY = 1.0
STEP_PRIMAL = 0.3
STEP_INVEST = 0.5
STEP_DUAL = 0.3
STEP_CAP = 0.05

F32 = jnp.float32
BF16 = jnp.bfloat16
COL_TILE = 256
VMEM_LIMIT = 24 * 1024 * 1024

IN_VMEM = pl.BlockSpec(memory_space=pltpu.VMEM)
IN_SMEM = pl.BlockSpec(memory_space=pltpu.SMEM)
IN_HBM = pl.BlockSpec(memory_space=pltpu.HBM)


def call(body, outs, args, arg_specs=None, out_specs=None, scratch=(), aliases=None, flops=0):
    if arg_specs is not None:
        args = [
            pltpu.with_memory_space_constraint(a, pltpu.HBM) if spec is IN_HBM else a
            for a, spec in zip(args, arg_specs)
        ]
    bytes_moved = sum(a.size * a.dtype.itemsize for a in args)
    bytes_moved += sum(math.prod(o.shape) * jnp.dtype(o.dtype).itemsize for o in outs)
    return pl.pallas_call(
        body,
        out_shape=tuple(outs),
        in_specs=arg_specs or [IN_VMEM] * len(args),
        out_specs=out_specs or tuple(IN_VMEM for _ in outs),
        scratch_shapes=list(scratch),
        input_output_aliases=aliases or {},
        compiler_params=pltpu.CompilerParams(vmem_limit_bytes=VMEM_LIMIT),
        cost_estimate=pl.CostEstimate(flops=flops, bytes_accessed=bytes_moved, transcendentals=0),
    )(*args)


def shape(dims, dtype=F32):
    return jax.ShapeDtypeStruct(tuple(dims), dtype)


def in_vmem(dims, dtype=F32):
    return pltpu.VMEM(tuple(dims), dtype)


def tiles(width):
    return [
        (half, slice(at, at + COL_TILE), slice(half * width + at, half * width + at + COL_TILE))
        for half in range(2)
        for at in range(0, width, COL_TILE)
    ]


def run_copies(pairs, sems):
    copies = [pltpu.make_async_copy(a, b, sems.at[i]) for i, (a, b) in enumerate(pairs)]
    for copy in copies:
        copy.start()
    for copy in copies:
        copy.wait()


def give_body(mine, *refs):
    *sources, out, sems = refs
    core = lax.rem(lax.axis_index("reg"), 2)
    given = pl.ds((1 - core) * mine, mine)
    run_copies([(src.at[given], out.at[i]) for i, src in enumerate(sources)], sems)


def held_body(mine, *refs):
    *sources, out, dual_out, dem_out, sems = refs
    core = lax.rem(lax.axis_index("reg"), 2)
    held = pl.ds(core * mine, mine)
    targets = [out.at[0], out.at[1], out.at[2], dual_out, dem_out]
    run_copies([(src.at[held], dst) for src, dst in zip(sources, targets)], sems)


def small_body(cost, mult, cons, capacity, own, give):
    sections = cost.shape[0]
    mine = own.shape[1]
    core = lax.rem(lax.axis_index("reg"), 2)
    for g in range(sections):
        const = cost[g:g + 1, :] + mult[g] - PENALTY * cons[g]
        for at, x in ((g, const), (sections + g, capacity[g])):
            own[at] = jnp.where(core == 0, x[:mine], x[mine:])
            give[at] = jnp.where(core == 0, x[mine:], x[:mine])


def matrix_body(tile, mask, out):
    out[...] = tile[0] * mask[0].astype(F32).astype(BF16)


def message_body(paired, own, twin, part, part_in, small, small_in, *outs):
    matrix, const, invest, near, far, mean = outs
    _, mine, _, width = own.shape
    sections = invest.shape[0]
    matrix[:, :width] = part[...]
    matrix[:, width:] = part_in[...]
    for src, cols in ((small, slice(0, width)), (small_in, slice(width, 2 * width))):
        const[:, :, cols] = src[:sections]
        invest[:, :, cols] = src[sections:]
    both = (own, twin)
    for s in range(mine):
        for half, cols, flat in tiles(width):
            src = both[half]
            write_message(paired, near, far, s, flat, src[1, s, :, cols], src[0, s, :, cols])
    mean[...] = near[:mine, :]


def is_odd():
    return lax.rem(lax.axis_index("hour"), 2) == 1


def write_message(paired, near, far, s, flat, c, x):
    mine = near.shape[0] // 2
    hours = x.shape[0]
    hour_sum = jnp.sum(c, axis=0, keepdims=True)
    near[pl.ds(s, 1), flat] = hour_sum
    far[pl.ds(s, 1), flat] = hour_sum
    first, last = x[0:1], x[hours - 1:hours]
    if paired:
        odd = is_odd()
        first, last = jnp.where(odd, last, first), jnp.where(odd, first, last)
    near[pl.ds(mine + s, 1), flat] = last
    far[pl.ds(mine + s, 1), flat] = first


def new_invest(hours_all, sums, invest, const):
    mine = invest.shape[1]
    parts = [part[:mine, :] for part in sums]
    while len(parts) > 1:
        parts = [u + v for u, v in zip(parts[0::2], parts[1::2])]
    mean = parts[0] / hours_all
    olds = [invest[g] for g in range(invest.shape[0])]
    news = [
        jnp.maximum(old - STEP_INVEST * (const[g] + PENALTY * old - mean), 0.0)
        for g, old in enumerate(olds)
    ]
    return olds, news


def invest_body(hours_all, sums_count, *refs):
    invest, const = refs[:2]
    keep, give = refs[2 + sums_count:]
    width = keep.shape[2]
    for g, new in enumerate(new_invest(hours_all, refs[2:2 + sums_count], invest, const)[1]):
        keep[g] = new[:, :width]
        give[g] = new[:, width:]


def primal_body(paired, first, last, *refs):
    refs = list(refs)
    take = lambda count: [refs.pop(0) for _ in range(count)]
    matrix, own, twin, dual, near, far = take(6)
    both = (own, twin)
    cost = [src.at[2] for src in both]
    if first:
        prim, cap = [src.at[0] for src in both], [src.at[1] for src in both]
    else:
        prim, cap = take(2), take(2)
        dem, sent, carry, received = take(4)
    prim_out = take(2)
    if last:
        base_out, rows_give = take(2)
    else:
        sent_out, carry_out = take(2)
        if not first:
            dual_out = take(1)[0]
    ext_low = take(1)[0]
    mine, hours, width = prim[0].shape
    chip = lax.axis_index("reg") // 2
    place = lax.axis_index("hour")
    has_prev = (place > 0).astype(F32)
    has_next = (place < lax.axis_size("hour") - 1).astype(F32)
    row = lax.broadcasted_iota(jnp.int32, (hours, COL_TILE), 0)
    for s in range(mine):
        multipliers = dual[s]
        if not first:
            image = sent[s].astype(F32) + received[s].astype(F32)
            multipliers = jnp.maximum(multipliers + STEP_DUAL * (dem[s] - image), 0.0)
            if not last:
                dual_out[s] = multipliers
        low = multipliers.astype(BF16)
        before = near[mine + s:mine + s + 1, :]
        after = far[mine + s:mine + s + 1, :]
        if paired:
            odd = is_odd()
            before, after = jnp.where(odd, before, after), jnp.where(odd, after, before)
        before = before * has_prev
        after = after * has_next
        for half, cols, flat in tiles(width):
            pulled = jnp.dot(low, matrix[:, flat], preferred_element_type=F32)
            x = prim[half][s, :, cols]
            prev = jnp.where(row == 0, before[:, flat], pltpu.roll(x, 1, 0))
            follow = jnp.where(row == hours - 1, after[:, flat], pltpu.roll(x, hours - 1, 0))
            rough = 2.0 * x - prev - follow
            c = cap[half][s, :, cols]
            grad = cost[half][s, :, cols] + RAMP_WEIGHT * rough - pulled + c
            new = jnp.maximum(x - STEP_PRIMAL * grad, 0.0)
            prim_out[half][s, :, cols] = new
            ext = 2.0 * new - x
            ext_low[:, flat] = ext.astype(BF16)
        total = lax.dot_general(
            ext_low[...], matrix[...], (((1,), (1,)), ((), ())), preferred_element_type=F32
        )
        if not first:
            total = total + carry[s]
        if last:
            rows = total.shape[1] // 2
            low_chip = chip == 0
            keep = jnp.where(low_chip, total[:, :rows], total[:, rows:])
            rows_give[s] = jnp.where(low_chip, total[:, rows:], total[:, :rows])
            base = multipliers + STEP_DUAL * dem[s]
            base_out[s] = jnp.where(low_chip, base[:, :rows], base[:, rows:]) - STEP_DUAL * keep
        else:
            low_sum = total.astype(BF16)
            sent_out[s] = low_sum
            carry_out[s] = total - low_sum.astype(F32)


def cap_body(hours_all, paired, sums_count, first, *refs):
    refs = list(refs)
    take = lambda count: [refs.pop(0) for _ in range(count)]
    if first:
        both = take(2)
        prim, cap = [src.at[0] for src in both], [src.at[1] for src in both]
    else:
        prim, cap = take(2), take(2)
    fresh = take(2)
    invest, const = take(2)
    sums = take(sums_count)
    cap_out = take(2)
    invest_out, near_out, far_out, mean_out = take(4)
    olds, news = new_invest(hours_all, sums, invest, const)
    limits = 0.0
    for g, (old, new) in enumerate(zip(olds, news)):
        invest_out[g] = new
        limits = limits + (2.0 * new - old)
    mine, _, width = prim[0].shape
    for s in range(mine):
        limit = limits[s:s + 1, :]
        for half, cols, flat in tiles(width):
            new = fresh[half][s, :, cols]
            ext = 2.0 * new - prim[half][s, :, cols]
            c = jnp.maximum(cap[half][s, :, cols] + STEP_CAP * (ext - limit[:, flat]), 0.0)
            cap_out[half][s, :, cols] = c
            write_message(paired, near_out, far_out, s, flat, c, new)
    mean_out[...] = near_out[:mine, :]


def join_body(*refs):
    kept, got, out, sems = refs
    mine = kept.shape[0]
    core = lax.rem(lax.axis_index("reg"), 2)
    run_copies(
        [(kept, out.at[pl.ds(core * mine, mine)]), (got, out.at[pl.ds((1 - core) * mine, mine)])],
        sems,
    )


def join(kept, got):
    mine = kept.shape[0]
    return call(
        join_body,
        (shape((2 * mine,) + kept.shape[1:]),),
        (kept, got),
        out_specs=(IN_HBM,),
        scratch=(pltpu.SemaphoreType.DMA((2,)),),
    )[0]


def dual_body(base, got, out, give, kept, sem):
    core = lax.rem(lax.axis_index("reg"), 2)
    mine, part = give.shape[:2]
    for s in range(mine):
        new = jnp.maximum(base[s] - STEP_DUAL * got[s], 0.0).T
        low, high = new[:part], new[part:]
        kept[s] = jnp.where(core == 0, low, high)
        give[s] = jnp.where(core == 0, high, low)
    run_copies([(kept, out.at[pl.ds(core * mine, mine)])], sem)


def rest_body(got, _, out, sem):
    core = lax.rem(lax.axis_index("reg"), 2)
    mine = got.shape[0]
    run_copies([(got, out.at[pl.ds((1 - core) * mine, mine)])], sem)


def node_weights(nodes, weights, g, s, n):
    return jnp.where(nodes[g, s] == n, weights[s], 0.0)


def nodes_body(node_count, keep, got, nodes, weights, capacity, packed):
    core = lax.rem(lax.axis_index("reg"), 2)
    sections, mine, width = keep.shape
    for g in range(sections):
        first = jnp.where(core == 0, keep[g], got[g])
        second = jnp.where(core == 0, got[g], keep[g])
        capacity[g, :mine] = first
        capacity[g, mine:] = second
        for n in range(node_count):
            total = jnp.zeros((1, width), F32)
            mass = jnp.zeros((1, 128), F32)
            for s in range(2 * mine):
                weight = node_weights(nodes, weights, g, s, n)
                row = first[s:s + 1] if s < mine else second[s - mine:s - mine + 1]
                total = total + weight * row
                mass = mass + weight
            packed[g, n:n + 1, :width] = total
            packed[g, n:n + 1, width:] = mass


def multiplier_body(mult, capacity, nodes, *refs):
    *packs, out = refs
    sections, scens, width = capacity.shape
    for g in range(sections):
        packed = packs[0][g]
        for other in packs[1:]:
            packed = packed + other[g]
        mass = packed[:, width:width + 1]
        average = packed[:, :width] / jnp.where(mass > 0.0, mass, 1.0)
        for s in range(scens):
            mine = jnp.zeros((1, width), F32)
            for n in range(packed.shape[0]):
                mine = mine + jnp.where(nodes[g, s] == n, average[n:n + 1], 0.0)
            out[g, s:s + 1] = mult[g, s:s + 1] + PENALTY * (capacity[g, s:s + 1] - mine)


def hour_exchange(near, far, mean, paired):
    count = lax.axis_size("hour")
    if not paired:
        near_in = lax.ppermute(near, "hour", [(i, (i + 1) % count) for i in range(count)])
        far_in = lax.ppermute(far, "hour", [((i + 1) % count, i) for i in range(count)])
        return near_in, far_in, (lax.psum(mean, "hour"),)
    partners = lambda by: [(i, i ^ by) for i in range(count)]
    far_in = lax.ppermute(far, "hour", partners(3))
    near_in = lax.ppermute(near, "hour", partners(1))
    across = lax.ppermute(mean, "hour", partners(2))
    return near_in, far_in, (mean, near_in, across, far_in)


def shards(
    cost_rate,
    invest_cost,
    tile,
    tile_mask,
    demand,
    dispatch,
    dual,
    cap_dual,
    capacity,
    multiplier,
    consensus,
    scen_weight,
    node_of,
):
    reg_count = lax.axis_size("reg")
    assert reg_count == 4
    paired = lax.axis_size("hour") == 4
    nscen, hours, width = dispatch.shape
    rows = dual.shape[2]
    mine = nscen // 2
    sections = capacity.shape[1]
    hours_all = float(hours * lax.axis_size("hour"))
    twin = [(i, i ^ 1) for i in range(reg_count)]
    other_chip = [(i, i ^ 2) for i in range(reg_count)]
    half_full = in_vmem((mine, hours, width))
    three = in_vmem((3, mine, hours, width))
    dual_like = in_vmem((mine, hours, rows))
    message = in_vmem((2 * mine, 2 * width))
    mean_like = in_vmem((mine, 2 * width))
    invest_like = in_vmem((sections, mine, 2 * width))
    small_like = in_vmem((2 * sections, mine, width))
    inv_half = in_vmem((sections, mine, width))
    by_section = lambda x: jnp.transpose(x, (1, 0, 2))
    mult, cons, caps = by_section(multiplier), by_section(consensus), by_section(capacity)

    (give,) = call(
        functools.partial(give_body, mine),
        (three,),
        (dispatch, cap_dual, cost_rate),
        arg_specs=[IN_HBM] * 3,
        scratch=(pltpu.SemaphoreType.DMA((3,)),),
    )
    twin_in = lax.ppermute(give, "reg", twin)
    (part,) = call(matrix_body, (in_vmem(tile.shape[1:], BF16),), (tile, tile_mask))
    part_in = lax.ppermute(part, "reg", twin)
    small, small_give = call(small_body, (small_like,) * 2, (invest_cost, mult, cons, caps))
    small_in = lax.ppermute(small_give, "reg", twin)
    own, dual_var, dem = call(
        functools.partial(held_body, mine),
        (three, dual_like, dual_like),
        (dispatch, cap_dual, cost_rate, dual, demand),
        arg_specs=[IN_HBM] * 5,
        scratch=(pltpu.SemaphoreType.DMA((5,)),),
    )
    matrix, const, invest, near, far, mean = call(
        functools.partial(message_body, paired),
        (in_vmem((rows, 2 * width), BF16), invest_like, invest_like, message, message, mean_like),
        (own, twin_in, part, part_in, small, small_in),
    )
    near_in, far_in, sums = hour_exchange(near, far, mean, paired)

    flops = 4 * mine * hours * rows * 2 * width
    prim = cap = ()
    sent = carry = received = None
    for step in range(ITERS):
        first, last = step == 0, step + 1 == ITERS
        args = [matrix, own, twin_in, dual_var, near_in, far_in, *prim, *cap]
        if not first:
            args += [dem, sent, carry, received]
        outs = [half_full] * 2
        if last:
            outs += [in_vmem((mine, hours, rows // 2))] * 2
        else:
            outs += [in_vmem((mine, hours, rows), BF16), dual_like]
            if not first:
                outs += [dual_like]
        got = call(
            functools.partial(primal_body, paired, first, last),
            outs,
            args,
            scratch=(pltpu.VMEM((hours, 2 * width), BF16),),
            flops=flops,
        )
        fresh = tuple(got[:2])
        if not last:
            sent, carry = got[2:4]
            received = lax.ppermute(sent, "reg", other_chip)
            if not first:
                dual_var = got[4]
            old = (own, twin_in) if first else (*prim, *cap)
            *cap, invest, near, far, mean = call(
                functools.partial(cap_body, hours_all, paired, len(sums), first),
                (half_full, half_full, invest_like, message, message, mean_like),
                (*old, *fresh, invest, const, *sums),
            )
            near_in, far_in, sums = hour_exchange(near, far, mean, paired)
            prim = fresh
            continue
        prim = fresh
        inv_keep, inv_give = call(
            functools.partial(invest_body, hours_all, len(sums)),
            (inv_half,) * 2,
            (invest, const, *sums),
        )
        inv_got = lax.ppermute(inv_give, "reg", twin)
        base, rows_give = got[2:]
        rows_got = lax.ppermute(rows_give, "reg", other_chip)
        prim_got = lax.ppermute(prim[1], "reg", twin)
        scen_count = lax.axis_size("scen")
        node_count = node_of.shape[1] * scen_count // 2
        packed_like = in_vmem((sections, node_count, width + 128))
        by_scen = in_vmem((sections, nscen, width))
        capacity_out, packed = call(
            functools.partial(nodes_body, node_count),
            (by_scen, packed_like),
            (inv_keep, inv_got, node_of, scen_weight),
            arg_specs=[IN_VMEM, IN_VMEM, IN_SMEM, IN_SMEM],
        )
        if scen_count == 2:
            packs = (packed, lax.ppermute(packed, "scen", [(0, 1), (1, 0)]))
        else:
            packs = (lax.psum(packed, "scen"),)
        (multiplier_out,) = call(
            multiplier_body,
            (by_scen,),
            (mult, capacity_out, node_of, *packs),
            arg_specs=[IN_VMEM, IN_VMEM, IN_SMEM] + [IN_VMEM] * len(packs),
        )
        dispatch_out = join(prim[0], prim_got)
        own_rows = rows // reg_count
        dual_half, dual_give = call(
            dual_body,
            (shape((nscen, own_rows, hours)), in_vmem((mine, own_rows, hours))),
            (base, rows_got),
            out_specs=(IN_HBM, IN_VMEM),
            scratch=(pltpu.VMEM((mine, own_rows, hours), F32), pltpu.SemaphoreType.DMA((1,))),
        )
        dual_got = lax.ppermute(dual_give, "reg", twin)
        (dual_out,) = call(
            rest_body,
            (shape(dual_half.shape),),
            (dual_got, dual_half),
            arg_specs=[IN_VMEM, IN_HBM],
            out_specs=(IN_HBM,),
            scratch=(pltpu.SemaphoreType.DMA((1,)),),
            aliases={1: 0},
        )
    return (
        dispatch_out,
        jnp.transpose(dual_out, (0, 2, 1)),
        by_section(capacity_out),
        by_section(multiplier_out),
    )


def solution(mesh):
    placed = (
        P("scen", "hour", "reg"),
        P(None, "reg"),
        P("hour", None, "reg"),
        P("hour", None, "reg"),
        P("scen", "hour", None),
        P("scen", "hour", "reg"),
        P("scen", "hour", None),
        P("scen", "hour", "reg"),
        P("scen", None, "reg"),
        P("scen", None, "reg"),
        P("scen", None, "reg"),
        P("scen"),
        P(None, "scen"),
    )
    return jax.shard_map(
        shards,
        mesh=mesh,
        in_specs=placed,
        out_specs=(
            P("scen", "hour", "reg"),
            P("scen", "hour", "reg"),
            P("scen", None, "reg"),
            P("scen", None, "reg"),
        ),
        check_vma=False,
    )
```

```python
import functools
import math

import jax
import jax.numpy as jnp
from jax import lax
from jax.experimental import pallas as pl
from jax.experimental.pallas import tpu as pltpu
from jax.sharding import PartitionSpec as P


ITERS = 8
RAMP_WEIGHT = 0.5
PENALTY = 1.0
STEP_PRIMAL = 0.3
STEP_INVEST = 0.5
STEP_DUAL = 0.3
STEP_CAP = 0.05

F32 = jnp.float32
BF16 = jnp.bfloat16
COL_TILE = 256
VMEM_LIMIT = 24 * 1024 * 1024

IN_VMEM = pl.BlockSpec(memory_space=pltpu.VMEM)
IN_SMEM = pl.BlockSpec(memory_space=pltpu.SMEM)
IN_HBM = pl.BlockSpec(memory_space=pltpu.HBM)


def call(body, outs, args, arg_specs=None, out_specs=None, scratch=(), aliases=None, flops=0):
    if arg_specs is not None:
        args = [
            pltpu.with_memory_space_constraint(a, pltpu.HBM) if spec is IN_HBM else a
            for a, spec in zip(args, arg_specs)
        ]
    bytes_moved = sum(a.size * a.dtype.itemsize for a in args)
    bytes_moved += sum(math.prod(o.shape) * jnp.dtype(o.dtype).itemsize for o in outs)
    return pl.pallas_call(
        body,
        out_shape=tuple(outs),
        in_specs=arg_specs or [IN_VMEM] * len(args),
        out_specs=out_specs or tuple(IN_VMEM for _ in outs),
        scratch_shapes=list(scratch),
        input_output_aliases=aliases or {},
        compiler_params=pltpu.CompilerParams(vmem_limit_bytes=VMEM_LIMIT),
        cost_estimate=pl.CostEstimate(flops=flops, bytes_accessed=bytes_moved, transcendentals=0),
    )(*args)


def shape(dims, dtype=F32):
    return jax.ShapeDtypeStruct(tuple(dims), dtype)


def in_vmem(dims, dtype=F32):
    return pltpu.VMEM(tuple(dims), dtype)


def tiles(width):
    return [
        (half, slice(at, at + COL_TILE), slice(half * width + at, half * width + at + COL_TILE))
        for half in range(2)
        for at in range(0, width, COL_TILE)
    ]


def run_copies(pairs, sems):
    copies = [pltpu.make_async_copy(a, b, sems.at[i]) for i, (a, b) in enumerate(pairs)]
    for copy in copies:
        copy.start()
    for copy in copies:
        copy.wait()


def give_body(mine, *refs):
    *sources, out, sems = refs
    core = lax.rem(lax.axis_index("reg"), 2)
    given = pl.ds((1 - core) * mine, mine)
    run_copies([(src.at[given], out.at[i]) for i, src in enumerate(sources)], sems)


def load_body(mine, cost, prim, cap, dual, dem, give, own, dual_out, dem_out, sems):
    core = lax.rem(lax.axis_index("reg"), 2)
    held = pl.ds(core * mine, mine)
    pairs = [(cost.at[pl.ds((1 - core) * mine, mine)], give)]
    targets = ((prim, own.at[0]), (cap, own.at[1]), (cost, own.at[2]), (dual, dual_out), (dem, dem_out))
    run_copies(pairs + [(src.at[held], dst) for src, dst in targets], sems)


def small_body(cost, mult, cons, capacity, own, give):
    sections = cost.shape[0]
    mine = own.shape[1]
    core = lax.rem(lax.axis_index("reg"), 2)
    for g in range(sections):
        const = cost[g:g + 1, :] + mult[g] - PENALTY * cons[g]
        for at, x in ((g, const), (sections + g, capacity[g])):
            own[at] = jnp.where(core == 0, x[:mine], x[mine:])
            give[at] = jnp.where(core == 0, x[mine:], x[:mine])


def matrix_body(tile, mask, out):
    out[...] = tile[0] * mask[0].astype(F32).astype(BF16)


def message_body(paired, own, twin, part, part_in, small, small_in, *outs):
    matrix, const, invest, near, far, mean = outs
    _, mine, _, width = own.shape
    sections = invest.shape[0]
    matrix[:, :width] = part[...]
    matrix[:, width:] = part_in[...]
    for src, cols in ((small, slice(0, width)), (small_in, slice(width, 2 * width))):
        const[:, :, cols] = src[:sections]
        invest[:, :, cols] = src[sections:]
    both = (own, twin)
    for s in range(mine):
        for half, cols, flat in tiles(width):
            src = both[half]
            write_message(paired, near, far, s, flat, src[1, s, :, cols], src[0, s, :, cols])
    mean[...] = near[:mine, :]


def is_odd():
    return lax.rem(lax.axis_index("hour"), 2) == 1


def write_message(paired, near, far, s, flat, c, x):
    mine = near.shape[0] // 2
    hours = x.shape[0]
    hour_sum = jnp.sum(c, axis=0, keepdims=True)
    near[pl.ds(s, 1), flat] = hour_sum
    far[pl.ds(s, 1), flat] = hour_sum
    first, last = x[0:1], x[hours - 1:hours]
    if paired:
        odd = is_odd()
        first, last = jnp.where(odd, last, first), jnp.where(odd, first, last)
    near[pl.ds(mine + s, 1), flat] = last
    far[pl.ds(mine + s, 1), flat] = first


def new_invest(hours_all, sums, invest, const):
    mine = invest.shape[1]
    parts = [part[:mine, :] for part in sums]
    while len(parts) > 1:
        parts = [u + v for u, v in zip(parts[0::2], parts[1::2])]
    mean = parts[0] / hours_all
    olds = [invest[g] for g in range(invest.shape[0])]
    news = [
        jnp.maximum(old - STEP_INVEST * (const[g] + PENALTY * old - mean), 0.0)
        for g, old in enumerate(olds)
    ]
    return olds, news


def invest_body(hours_all, sums_count, *refs):
    invest, const = refs[:2]
    keep, give = refs[2 + sums_count:]
    width = keep.shape[2]
    for g, new in enumerate(new_invest(hours_all, refs[2:2 + sums_count], invest, const)[1]):
        keep[g] = new[:, :width]
        give[g] = new[:, width:]


def primal_body(paired, first, last, *refs):
    refs = list(refs)
    take = lambda count: [refs.pop(0) for _ in range(count)]
    matrix, own, twin_cost, dual, near, far = take(6)
    cost = (own.at[2], twin_cost)
    if first:
        both = take(2)
        prim, cap = [src.at[0] for src in both], [src.at[1] for src in both]
    else:
        prim, cap = take(2), take(2)
        dem, sent, carry, received = take(4)
    prim_out = take(2)
    if last:
        base_out, rows_give = take(2)
    else:
        sent_out, carry_out = take(2)
        if not first:
            dual_out = take(1)[0]
    mine, hours, width = prim[0].shape
    chip = lax.axis_index("reg") // 2
    place = lax.axis_index("hour")
    has_prev = (place > 0).astype(F32)
    has_next = (place < lax.axis_size("hour") - 1).astype(F32)
    height = mine * hours
    row = lax.broadcasted_iota(jnp.int32, (height, COL_TILE), 0)
    flatten = lambda x: x.reshape(height, x.shape[-1])
    multipliers = flatten(dual[...])
    if not first:
        image = sent[...].astype(F32) + received[...].astype(F32)
        multipliers = jnp.maximum(multipliers + STEP_DUAL * flatten(dem[...] - image), 0.0)
        if not last:
            dual_out[...] = multipliers.reshape(dual_out.shape)
    low = multipliers.astype(BF16)
    before = near[mine:, :]
    after = far[mine:, :]
    if paired:
        odd = is_odd()
        before, after = jnp.where(odd, before, after), jnp.where(odd, after, before)
    before = before * has_prev
    after = after * has_next
    total = None if first else flatten(carry[...])
    for half, cols, flat in tiles(width):
        pulled = jnp.dot(low, matrix[:, flat], preferred_element_type=F32)
        x = flatten(prim[half][:, :, cols])
        prev = pltpu.roll(x, 1, 0)
        follow = pltpu.roll(x, height - 1, 0)
        for s in range(mine):
            prev = jnp.where(row == s * hours, before[s:s + 1, flat], prev)
            follow = jnp.where(row == (s + 1) * hours - 1, after[s:s + 1, flat], follow)
        rough = 2.0 * x - prev - follow
        grad = flatten(cost[half][:, :, cols]) + RAMP_WEIGHT * rough - pulled
        grad = grad + flatten(cap[half][:, :, cols])
        new = jnp.maximum(x - STEP_PRIMAL * grad, 0.0)
        prim_out[half][:, :, cols] = new.reshape(mine, hours, COL_TILE)
        ext = (2.0 * new - x).astype(BF16)
        sums = lax.dot_general(
            ext, matrix[:, flat], (((1,), (1,)), ((), ())), preferred_element_type=F32
        )
        total = sums if total is None else total + sums
    split = lambda x: x.reshape(mine, hours, x.shape[-1])
    if last:
        rows = total.shape[1] // 2
        low_chip = chip == 0
        keep = jnp.where(low_chip, total[:, :rows], total[:, rows:])
        rows_give[...] = split(jnp.where(low_chip, total[:, rows:], total[:, :rows]))
        base = multipliers + STEP_DUAL * flatten(dem[...])
        base_out[...] = split(jnp.where(low_chip, base[:, :rows], base[:, rows:]) - STEP_DUAL * keep)
    else:
        low_sum = total.astype(BF16)
        sent_out[...] = split(low_sum.astype(F32)).astype(BF16)
        carry_out[...] = split(total - low_sum.astype(F32))


def cap_body(hours_all, paired, sums_count, first, *refs):
    refs = list(refs)
    take = lambda count: [refs.pop(0) for _ in range(count)]
    if first:
        both = take(2)
        prim, cap = [src.at[0] for src in both], [src.at[1] for src in both]
    else:
        prim, cap = take(2), take(2)
    fresh = take(2)
    invest, const = take(2)
    sums = take(sums_count)
    cap_out = take(2)
    invest_out, near_out, far_out, mean_out = take(4)
    olds, news = new_invest(hours_all, sums, invest, const)
    limits = 0.0
    for g, (old, new) in enumerate(zip(olds, news)):
        invest_out[g] = new
        limits = limits + (2.0 * new - old)
    mine, _, width = prim[0].shape
    for s in range(mine):
        limit = limits[s:s + 1, :]
        for half, cols, flat in tiles(width):
            new = fresh[half][s, :, cols]
            ext = 2.0 * new - prim[half][s, :, cols]
            c = jnp.maximum(cap[half][s, :, cols] + STEP_CAP * (ext - limit[:, flat]), 0.0)
            cap_out[half][s, :, cols] = c
            write_message(paired, near_out, far_out, s, flat, c, new)
    mean_out[...] = near_out[:mine, :]


def join_body(*refs):
    kept, got, out, sems = refs
    mine = kept.shape[0]
    core = lax.rem(lax.axis_index("reg"), 2)
    run_copies(
        [(kept, out.at[pl.ds(core * mine, mine)]), (got, out.at[pl.ds((1 - core) * mine, mine)])],
        sems,
    )


def join(kept, got):
    mine = kept.shape[0]
    return call(
        join_body,
        (shape((2 * mine,) + kept.shape[1:]),),
        (kept, got),
        out_specs=(IN_HBM,),
        scratch=(pltpu.SemaphoreType.DMA((2,)),),
    )[0]


def dual_body(base, got, keep, give):
    core = lax.rem(lax.axis_index("reg"), 2)
    mine, part = give.shape[:2]
    for s in range(mine):
        new = jnp.maximum(base[s] - STEP_DUAL * got[s], 0.0).T
        low, high = new[:part], new[part:]
        keep[s] = jnp.where(core == 0, low, high)
        give[s] = jnp.where(core == 0, high, low)


def member_body(nodes, weights, hot, weighted):
    sections, count, scens, lanes = hot.shape
    one, zero = jnp.ones((1, lanes), F32), jnp.zeros((1, lanes), F32)
    for g in range(sections):
        for n in range(count):
            for s in range(scens):
                held = jnp.where(nodes[g, s] == n, one, zero)
                hot[g, n, s:s + 1] = held
                weighted[g, n, s:s + 1] = held * weights[s]


def widen(x, width):
    return jnp.concatenate([x] * (width // x.shape[-1]), axis=-1)


def nodes_body(keep, got, weighted, capacity, packed):
    core = lax.rem(lax.axis_index("reg"), 2)
    sections, mine, width = keep.shape
    for g in range(sections):
        capacity[g, :mine] = jnp.where(core == 0, keep[g], got[g])
        capacity[g, mine:] = jnp.where(core == 0, got[g], keep[g])
        built = capacity[g]
        for n in range(packed.shape[1]):
            weight = weighted[g, n]
            packed[g, n:n + 1, :width] = jnp.sum(widen(weight, width) * built, axis=0, keepdims=True)
            packed[g, n:n + 1, width:] = jnp.sum(weight, axis=0, keepdims=True)


def finish_body(packs_count, *refs):
    kept, got, mult, capacity, hot = refs[:5]
    packs = refs[5:5 + packs_count]
    dual_out, capacity_out, mult_out, mult_new, sems = refs[5 + packs_count:]
    core = lax.rem(lax.axis_index("reg"), 2)
    sections, scens, width = capacity.shape
    mine = scens // 2
    copies = [
        pltpu.make_async_copy(kept, dual_out.at[pl.ds(core * mine, mine)], sems.at[0]),
        pltpu.make_async_copy(got, dual_out.at[pl.ds((1 - core) * mine, mine)], sems.at[1]),
        pltpu.make_async_copy(capacity, capacity_out, sems.at[2]),
        pltpu.make_async_copy(mult_new, mult_out, sems.at[3]),
    ]
    for copy in copies[:3]:
        copy.start()
    for g in range(sections):
        packed = packs[0][g]
        for other in packs[1:]:
            packed = packed + other[g]
        mass = packed[:, width:width + 1]
        average = packed[:, :width] / jnp.where(mass > 0.0, mass, 1.0)
        back = jnp.zeros((scens, width), F32)
        for n in range(packed.shape[0]):
            back = back + widen(hot[g, n], width) * average[n:n + 1]
        mult_new[g] = mult[g] + PENALTY * (capacity[g] - back)
    copies[3].start()
    for copy in copies:
        copy.wait()


def hour_exchange(near, far, mean, paired):
    count = lax.axis_size("hour")
    if not paired:
        near_in = lax.ppermute(near, "hour", [(i, (i + 1) % count) for i in range(count)])
        far_in = lax.ppermute(far, "hour", [((i + 1) % count, i) for i in range(count)])
        return near_in, far_in, (lax.psum(mean, "hour"),)
    partners = lambda by: [(i, i ^ by) for i in range(count)]
    far_in = lax.ppermute(far, "hour", partners(3))
    near_in = lax.ppermute(near, "hour", partners(1))
    across = lax.ppermute(mean, "hour", partners(2))
    return near_in, far_in, (mean, near_in, across, far_in)


def shards(
    cost_rate,
    invest_cost,
    tile,
    tile_mask,
    demand,
    dispatch,
    dual,
    cap_dual,
    capacity,
    multiplier,
    consensus,
    scen_weight,
    node_of,
):
    reg_count = lax.axis_size("reg")
    assert reg_count == 4
    paired = lax.axis_size("hour") == 4
    nscen, hours, width = dispatch.shape
    rows = dual.shape[2]
    mine = nscen // 2
    sections = capacity.shape[1]
    hours_all = float(hours * lax.axis_size("hour"))
    twin = [(i, i ^ 1) for i in range(reg_count)]
    other_chip = [(i, i ^ 2) for i in range(reg_count)]
    half_full = in_vmem((mine, hours, width))
    three = in_vmem((3, mine, hours, width))
    dual_like = in_vmem((mine, hours, rows))
    message = in_vmem((2 * mine, 2 * width))
    mean_like = in_vmem((mine, 2 * width))
    invest_like = in_vmem((sections, mine, 2 * width))
    small_like = in_vmem((2 * sections, mine, width))
    inv_half = in_vmem((sections, mine, width))
    by_section = lambda x: jnp.transpose(x, (1, 0, 2))
    mult, cons, caps = by_section(multiplier), by_section(consensus), by_section(capacity)

    (give,) = call(
        functools.partial(give_body, mine),
        (in_vmem((2, mine, hours, width)),),
        (dispatch, cap_dual),
        arg_specs=[IN_HBM] * 2,
        scratch=(pltpu.SemaphoreType.DMA((2,)),),
    )
    twin_state = lax.ppermute(give, "reg", twin)
    (part,) = call(matrix_body, (in_vmem(tile.shape[1:], BF16),), (tile, tile_mask))
    part_in = lax.ppermute(part, "reg", twin)
    small, small_give = call(small_body, (small_like,) * 2, (invest_cost, mult, cons, caps))
    small_in = lax.ppermute(small_give, "reg", twin)
    cost_give, own, dual_var, dem = call(
        functools.partial(load_body, mine),
        (half_full, three, dual_like, dual_like),
        (cost_rate, dispatch, cap_dual, dual, demand),
        arg_specs=[IN_HBM] * 5,
        scratch=(pltpu.SemaphoreType.DMA((6,)),),
    )
    twin_cost = lax.ppermute(cost_give, "reg", twin)
    matrix, const, invest, near, far, mean = call(
        functools.partial(message_body, paired),
        (in_vmem((rows, 2 * width), BF16), invest_like, invest_like, message, message, mean_like),
        (own, twin_state, part, part_in, small, small_in),
    )
    near_in, far_in, sums = hour_exchange(near, far, mean, paired)

    scen_count = lax.axis_size("scen")
    node_count = node_of.shape[1] * scen_count // 2
    flops = 4 * mine * hours * rows * 2 * width
    prim = cap = ()
    sent = carry = received = None
    for step in range(ITERS):
        first, last = step == 0, step + 1 == ITERS
        state = (own, twin_state) if first else (*prim, *cap)
        args = [matrix, own, twin_cost, dual_var, near_in, far_in, *state]
        if not first:
            args += [dem, sent, carry, received]
        outs = [half_full] * 2
        if last:
            outs += [in_vmem((mine, hours, rows // 2))] * 2
        else:
            outs += [in_vmem((mine, hours, rows), BF16), dual_like]
            if not first:
                outs += [dual_like]
        got = call(functools.partial(primal_body, paired, first, last), outs, args, flops=flops)
        fresh = tuple(got[:2])
        if not last:
            sent, carry = got[2:4]
            received = lax.ppermute(sent, "reg", other_chip)
            if not first:
                dual_var = got[4]
            *cap, invest, near, far, mean = call(
                functools.partial(cap_body, hours_all, paired, len(sums), first),
                (half_full, half_full, invest_like, message, message, mean_like),
                (*state, *fresh, invest, const, *sums),
            )
            near_in, far_in, sums = hour_exchange(near, far, mean, paired)
            if step == ITERS // 2:
                member_like = in_vmem((sections, node_count, nscen, 128))
                hot, weighted = call(
                    member_body,
                    (member_like, member_like),
                    (node_of, scen_weight),
                    arg_specs=[IN_SMEM, IN_SMEM],
                )
            prim = fresh
            continue
        prim = fresh
        inv_keep, inv_give = call(
            functools.partial(invest_body, hours_all, len(sums)),
            (inv_half,) * 2,
            (invest, const, *sums),
        )
        inv_got = lax.ppermute(inv_give, "reg", twin)
        base, rows_give = got[2:]
        rows_got = lax.ppermute(rows_give, "reg", other_chip)
        prim_got = lax.ppermute(prim[1], "reg", twin)
        capacity_all, packed = call(
            nodes_body,
            (in_vmem((sections, nscen, width)), in_vmem((sections, node_count, width + 128))),
            (inv_keep, inv_got, weighted),
        )
        if scen_count == 2:
            packs = (packed, lax.ppermute(packed, "scen", [(0, 1), (1, 0)]))
        else:
            packs = (lax.psum(packed, "scen"),)
        dispatch_out = join(prim[0], prim_got)
        own_rows = rows // reg_count
        dual_keep, dual_give = call(
            dual_body, (in_vmem((mine, own_rows, hours)),) * 2, (base, rows_got)
        )
        dual_got = lax.ppermute(dual_give, "reg", twin)
        dual_out, capacity_out, multiplier_out = call(
            functools.partial(finish_body, len(packs)),
            (
                pltpu.HBM((nscen, own_rows, hours), F32),
                pltpu.HBM((sections, nscen, width), F32),
                pltpu.HBM((sections, nscen, width), F32),
            ),
            (dual_keep, dual_got, mult, capacity_all, hot, *packs),
            out_specs=(IN_HBM,) * 3,
            scratch=(pltpu.VMEM((sections, nscen, width), F32), pltpu.SemaphoreType.DMA((4,))),
        )
    return (
        dispatch_out,
        jnp.transpose(dual_out, (0, 2, 1)),
        by_section(capacity_out),
        by_section(multiplier_out),
    )


def solution(mesh):
    placed = (
        P("scen", "hour", "reg"),
        P(None, "reg"),
        P("hour", None, "reg"),
        P("hour", None, "reg"),
        P("scen", "hour", None),
        P("scen", "hour", "reg"),
        P("scen", "hour", None),
        P("scen", "hour", "reg"),
        P("scen", None, "reg"),
        P("scen", None, "reg"),
        P("scen", None, "reg"),
        P("scen"),
        P(None, "scen"),
    )
    return jax.shard_map(
        shards,
        mesh=mesh,
        in_specs=placed,
        out_specs=(
            P("scen", "hour", "reg"),
            P("scen", "hour", "reg"),
            P("scen", None, "reg"),
            P("scen", None, "reg"),
        ),
        check_vma=False,
    )
```

```python
import functools
import math

import jax
import jax.numpy as jnp
from jax import lax
from jax.experimental import pallas as pl
from jax.experimental.pallas import tpu as pltpu
from jax.sharding import PartitionSpec as P


ITERS = 8
RAMP_WEIGHT = 0.5
PENALTY = 1.0
STEP_PRIMAL = 0.3
STEP_INVEST = 0.5
STEP_DUAL = 0.3
STEP_CAP = 0.05

F32 = jnp.float32
BF16 = jnp.bfloat16
COL_TILE = 256
VMEM_LIMIT = 24 * 1024 * 1024

IN_VMEM = pl.BlockSpec(memory_space=pltpu.VMEM)
IN_SMEM = pl.BlockSpec(memory_space=pltpu.SMEM)
IN_HBM = pl.BlockSpec(memory_space=pltpu.HBM)


def call(body, outs, args, arg_specs=None, out_specs=None, scratch=(), aliases=None, flops=0):
    if arg_specs is not None:
        args = [
            pltpu.with_memory_space_constraint(a, pltpu.HBM) if spec is IN_HBM else a
            for a, spec in zip(args, arg_specs)
        ]
    bytes_moved = sum(a.size * a.dtype.itemsize for a in args)
    bytes_moved += sum(math.prod(o.shape) * jnp.dtype(o.dtype).itemsize for o in outs)
    return pl.pallas_call(
        body,
        out_shape=tuple(outs),
        in_specs=arg_specs or [IN_VMEM] * len(args),
        out_specs=out_specs or tuple(IN_VMEM for _ in outs),
        scratch_shapes=list(scratch),
        input_output_aliases=aliases or {},
        compiler_params=pltpu.CompilerParams(vmem_limit_bytes=VMEM_LIMIT),
        cost_estimate=pl.CostEstimate(flops=flops, bytes_accessed=bytes_moved, transcendentals=0),
    )(*args)


def shape(dims, dtype=F32):
    return jax.ShapeDtypeStruct(tuple(dims), dtype)


def in_vmem(dims, dtype=F32):
    return pltpu.VMEM(tuple(dims), dtype)


def tiles(width):
    return [
        (half, slice(at, at + COL_TILE), slice(half * width + at, half * width + at + COL_TILE))
        for half in range(2)
        for at in range(0, width, COL_TILE)
    ]


def run_copies(pairs, sems):
    copies = [pltpu.make_async_copy(a, b, sems.at[i]) for i, (a, b) in enumerate(pairs)]
    for copy in copies:
        copy.start()
    for copy in copies:
        copy.wait()


def give_body(mine, *refs):
    *sources, out, sems = refs
    core = lax.rem(lax.axis_index("reg"), 2)
    given = pl.ds((1 - core) * mine, mine)
    run_copies([(src.at[given], out.at[i]) for i, src in enumerate(sources)], sems)


def load_body(mine, cost, prim, cap, dual, dem, give, own, dual_out, dem_out, sems):
    core = lax.rem(lax.axis_index("reg"), 2)
    held = pl.ds(core * mine, mine)
    pairs = [(cost.at[pl.ds((1 - core) * mine, mine)], give)]
    targets = ((prim, own.at[0]), (cap, own.at[1]), (cost, own.at[2]), (dual, dual_out), (dem, dem_out))
    run_copies(pairs + [(src.at[held], dst) for src, dst in targets], sems)


def small_body(cost, mult, cons, capacity, own, give):
    sections = cost.shape[0]
    mine = own.shape[1]
    core = lax.rem(lax.axis_index("reg"), 2)
    for g in range(sections):
        const = cost[g:g + 1, :] + mult[g] - PENALTY * cons[g]
        for at, x in ((g, const), (sections + g, capacity[g])):
            own[at] = jnp.where(core == 0, x[:mine], x[mine:])
            give[at] = jnp.where(core == 0, x[mine:], x[:mine])


def matrix_body(tile, mask, out):
    out[...] = tile[0] * mask[0].astype(F32).astype(BF16)


def message_body(paired, own, twin, part, part_in, small, small_in, *outs):
    matrix, turned, const, invest, near, far, mean = outs
    _, mine, _, width = own.shape
    sections = invest.shape[0]
    for half, src in enumerate((part, part_in)):
        cols = slice(half * width, (half + 1) * width)
        matrix[:, cols] = src[...]
        turned[cols, :] = src[...].T
    for src, cols in ((small, slice(0, width)), (small_in, slice(width, 2 * width))):
        const[:, :, cols] = src[:sections]
        invest[:, :, cols] = src[sections:]
    both = (own, twin)
    for s in range(mine):
        for half, cols, flat in tiles(width):
            src = both[half]
            write_message(paired, near, far, s, flat, src[1, s, :, cols], src[0, s, :, cols])
    mean[...] = near[:mine, :]


def is_odd():
    return lax.rem(lax.axis_index("hour"), 2) == 1


def write_message(paired, near, far, s, flat, c, x):
    mine = near.shape[0] // 2
    hours = x.shape[0]
    hour_sum = jnp.sum(c, axis=0, keepdims=True)
    near[pl.ds(s, 1), flat] = hour_sum
    far[pl.ds(s, 1), flat] = hour_sum
    first, last = x[0:1], x[hours - 1:hours]
    if paired:
        odd = is_odd()
        first, last = jnp.where(odd, last, first), jnp.where(odd, first, last)
    near[pl.ds(mine + s, 1), flat] = last
    far[pl.ds(mine + s, 1), flat] = first


def new_invest(hours_all, sums, invest, const):
    mine = invest.shape[1]
    parts = [part[:mine, :] for part in sums]
    if len(parts) > 1:
        place = lax.axis_index("hour")
        at_end = jnp.logical_or(place == 0, place == lax.axis_size("hour") - 1)
        parts[3:] = [jnp.where(at_end, parts[4], parts[3])]
    while len(parts) > 1:
        parts = [u + v for u, v in zip(parts[0::2], parts[1::2])]
    mean = parts[0] / hours_all
    olds = [invest[g] for g in range(invest.shape[0])]
    news = [
        jnp.maximum(old - STEP_INVEST * (const[g] + PENALTY * old - mean), 0.0)
        for g, old in enumerate(olds)
    ]
    return olds, news


def invest_body(hours_all, sums_count, *refs):
    invest, const = refs[:2]
    keep, give = refs[2 + sums_count:]
    width = keep.shape[2]
    for g, new in enumerate(new_invest(hours_all, refs[2:2 + sums_count], invest, const)[1]):
        keep[g] = new[:, :width]
        give[g] = new[:, width:]


def patch(x, rows, at, hours):
    start = at // 8 * 8
    row = lax.broadcasted_iota(jnp.int32, (8, x.shape[1]), 0)
    pieces = []
    for s in range(rows.shape[0]):
        base = s * hours
        pieces.append(x[base:base + start])
        pieces.append(jnp.where(row == at - start, rows[s:s + 1], x[base + start:base + start + 8]))
        pieces.append(x[base + start + 8:base + hours])
    return jnp.concatenate([p for p in pieces if p.shape[0]], axis=0)


def primal_body(paired, first, last, *refs):
    refs = list(refs)
    take = lambda count: [refs.pop(0) for _ in range(count)]
    matrix, turned, own, twin_cost, dual, near, far = take(7)
    cost = (own.at[2], twin_cost)
    if first:
        both = take(2)
        prim, cap = [src.at[0] for src in both], [src.at[1] for src in both]
    else:
        prim, cap = take(2), take(2)
        dem, sent, carry, received = take(4)
    prim_out = take(2)
    if last:
        base_out, rows_give = take(2)
    else:
        sent_out, carry_out = take(2)
        if not first:
            dual_out = take(1)[0]
    mine, hours, width = prim[0].shape
    chip = lax.axis_index("reg") // 2
    place = lax.axis_index("hour")
    has_prev = (place > 0).astype(F32)
    has_next = (place < lax.axis_size("hour") - 1).astype(F32)
    height = mine * hours
    flatten = lambda x: x.reshape(height, x.shape[-1])
    multipliers = flatten(dual[...])
    if not first:
        image = sent[...].astype(F32) + received[...].astype(F32)
        multipliers = jnp.maximum(multipliers + STEP_DUAL * flatten(dem[...] - image), 0.0)
        if not last:
            dual_out[...] = multipliers.reshape(dual_out.shape)
    low = multipliers.astype(BF16)
    before = near[mine:, :]
    after = far[mine:, :]
    if paired:
        odd = is_odd()
        before, after = jnp.where(odd, before, after), jnp.where(odd, after, before)
    before = before * has_prev
    after = after * has_next
    total = None if first else flatten(carry[...])
    for half, cols, flat in tiles(width):
        pulled = jnp.dot(low, matrix[:, flat], preferred_element_type=F32)
        x = flatten(prim[half][:, :, cols])
        prev = pltpu.roll(x, 1, 0)
        follow = pltpu.roll(x, height - 1, 0)
        prev = patch(prev, before[:, flat], 0, hours)
        follow = patch(follow, after[:, flat], hours - 1, hours)
        rough = 2.0 * x - prev - follow
        grad = flatten(cost[half][:, :, cols]) + RAMP_WEIGHT * rough - pulled
        grad = grad + flatten(cap[half][:, :, cols])
        new = jnp.maximum(x - STEP_PRIMAL * grad, 0.0)
        prim_out[half][:, :, cols] = new.reshape(mine, hours, COL_TILE)
        ext = (2.0 * new - x).astype(BF16)
        sums = jnp.dot(ext, turned[flat, :], preferred_element_type=F32)
        total = sums if total is None else total + sums
    split = lambda x: x.reshape(mine, hours, x.shape[-1])
    if last:
        rows = total.shape[1] // 2
        low_chip = chip == 0
        keep = jnp.where(low_chip, total[:, :rows], total[:, rows:])
        rows_give[...] = split(jnp.where(low_chip, total[:, rows:], total[:, :rows]))
        base = multipliers + STEP_DUAL * flatten(dem[...])
        base_out[...] = split(jnp.where(low_chip, base[:, :rows], base[:, rows:]) - STEP_DUAL * keep)
    else:
        low_sum = total.astype(BF16)
        sent_out[...] = split(low_sum.astype(F32)).astype(BF16)
        carry_out[...] = split(total - low_sum.astype(F32))


def cap_body(hours_all, paired, sums_count, first, *refs):
    refs = list(refs)
    take = lambda count: [refs.pop(0) for _ in range(count)]
    if first:
        both = take(2)
        prim, cap = [src.at[0] for src in both], [src.at[1] for src in both]
    else:
        prim, cap = take(2), take(2)
    fresh = take(2)
    invest, const = take(2)
    sums = take(sums_count)
    cap_out = take(2)
    invest_out, near_out, far_out, mean_out = take(4)
    olds, news = new_invest(hours_all, sums, invest, const)
    limits = 0.0
    for g, (old, new) in enumerate(zip(olds, news)):
        invest_out[g] = new
        limits = limits + (2.0 * new - old)
    mine, _, width = prim[0].shape
    for s in range(mine):
        limit = limits[s:s + 1, :]
        for half, cols, flat in tiles(width):
            new = fresh[half][s, :, cols]
            ext = 2.0 * new - prim[half][s, :, cols]
            c = jnp.maximum(cap[half][s, :, cols] + STEP_CAP * (ext - limit[:, flat]), 0.0)
            cap_out[half][s, :, cols] = c
            write_message(paired, near_out, far_out, s, flat, c, new)
    mean_out[...] = near_out[:mine, :]


def join_body(*refs):
    kept, got, out, sems = refs
    mine = kept.shape[0]
    core = lax.rem(lax.axis_index("reg"), 2)
    run_copies(
        [(kept, out.at[pl.ds(core * mine, mine)]), (got, out.at[pl.ds((1 - core) * mine, mine)])],
        sems,
    )


def join(kept, got):
    mine = kept.shape[0]
    return call(
        join_body,
        (shape((2 * mine,) + kept.shape[1:]),),
        (kept, got),
        out_specs=(IN_HBM,),
        scratch=(pltpu.SemaphoreType.DMA((2,)),),
    )[0]


def dual_body(base, got, keep, give):
    core = lax.rem(lax.axis_index("reg"), 2)
    mine, part = give.shape[:2]
    for s in range(mine):
        new = jnp.maximum(base[s] - STEP_DUAL * got[s], 0.0).T
        low, high = new[:part], new[part:]
        keep[s] = jnp.where(core == 0, low, high)
        give[s] = jnp.where(core == 0, high, low)


def member_body(nodes, weights, hot, weighted):
    sections, count, scens, lanes = hot.shape
    one, zero = jnp.ones((1, lanes), F32), jnp.zeros((1, lanes), F32)
    for g in range(sections):
        for n in range(count):
            for s in range(scens):
                held = jnp.where(nodes[g, s] == n, one, zero)
                hot[g, n, s:s + 1] = held
                weighted[g, n, s:s + 1] = held * weights[s]


def widen(x, width):
    return jnp.concatenate([x] * (width // x.shape[-1]), axis=-1)


def nodes_body(keep, got, weighted, capacity, packed):
    core = lax.rem(lax.axis_index("reg"), 2)
    sections, mine, width = keep.shape
    for g in range(sections):
        capacity[g, :mine] = jnp.where(core == 0, keep[g], got[g])
        capacity[g, mine:] = jnp.where(core == 0, got[g], keep[g])
        built = capacity[g]
        for n in range(packed.shape[1]):
            weight = weighted[g, n]
            packed[g, n:n + 1, :width] = jnp.sum(widen(weight, width) * built, axis=0, keepdims=True)
            packed[g, n:n + 1, width:] = jnp.sum(weight, axis=0, keepdims=True)


def finish_body(packs_count, *refs):
    kept, got, mult, capacity, hot = refs[:5]
    packs = refs[5:5 + packs_count]
    dual_out, capacity_out, mult_out, mult_new, sems = refs[5 + packs_count:]
    core = lax.rem(lax.axis_index("reg"), 2)
    sections, scens, width = capacity.shape
    mine = scens // 2
    copies = [
        pltpu.make_async_copy(kept, dual_out.at[pl.ds(core * mine, mine)], sems.at[0]),
        pltpu.make_async_copy(got, dual_out.at[pl.ds((1 - core) * mine, mine)], sems.at[1]),
        pltpu.make_async_copy(capacity, capacity_out, sems.at[2]),
        pltpu.make_async_copy(mult_new, mult_out, sems.at[3]),
    ]
    for copy in copies[:3]:
        copy.start()
    for g in range(sections):
        packed = packs[0][g]
        for other in packs[1:]:
            packed = packed + other[g]
        mass = packed[:, width:width + 1]
        average = packed[:, :width] / jnp.where(mass > 0.0, mass, 1.0)
        back = jnp.zeros((scens, width), F32)
        for n in range(packed.shape[0]):
            back = back + widen(hot[g, n], width) * average[n:n + 1]
        mult_new[g] = mult[g] + PENALTY * (capacity[g] - back)
    copies[3].start()
    for copy in copies:
        copy.wait()


def hour_exchange(near, far, mean, paired):
    count = lax.axis_size("hour")
    if not paired:
        near_in = lax.ppermute(near, "hour", [(i, (i + 1) % count) for i in range(count)])
        far_in = lax.ppermute(far, "hour", [((i + 1) % count, i) for i in range(count)])
        return near_in, far_in, (lax.psum(mean, "hour"),)
    reg_count = lax.axis_size("reg")
    partners = lambda by: [(i, i ^ by) for i in range(count)]
    place = lambda z, r: z * reg_count + r
    mirror = lambda places: [
        (place(z, r), place(count - 1 - z, r) if z in places else place(z, r ^ 1))
        for z in range(count)
        for r in range(reg_count)
    ]
    near_in = lax.ppermute(near, "hour", partners(1))
    far_in = lax.ppermute(mean, ("hour", "reg"), mirror((0, count - 1)))
    mid_in = lax.ppermute(far, ("hour", "reg"), mirror(range(1, count - 1)))
    across = lax.ppermute(mean, "hour", partners(2))
    return near_in, mid_in, (mean, near_in, across, mid_in, far_in)


def shards(
    cost_rate,
    invest_cost,
    tile,
    tile_mask,
    demand,
    dispatch,
    dual,
    cap_dual,
    capacity,
    multiplier,
    consensus,
    scen_weight,
    node_of,
):
    reg_count = lax.axis_size("reg")
    assert reg_count == 4
    paired = lax.axis_size("hour") == 4
    nscen, hours, width = dispatch.shape
    rows = dual.shape[2]
    mine = nscen // 2
    sections = capacity.shape[1]
    hours_all = float(hours * lax.axis_size("hour"))
    twin = [(i, i ^ 1) for i in range(reg_count)]
    other_chip = [(i, i ^ 2) for i in range(reg_count)]
    half_full = in_vmem((mine, hours, width))
    three = in_vmem((3, mine, hours, width))
    dual_like = in_vmem((mine, hours, rows))
    message = in_vmem((2 * mine, 2 * width))
    mean_like = in_vmem((mine, 2 * width))
    invest_like = in_vmem((sections, mine, 2 * width))
    small_like = in_vmem((2 * sections, mine, width))
    inv_half = in_vmem((sections, mine, width))
    by_section = lambda x: jnp.transpose(x, (1, 0, 2))
    mult, cons, caps = by_section(multiplier), by_section(consensus), by_section(capacity)

    (give,) = call(
        functools.partial(give_body, mine),
        (in_vmem((2, mine, hours, width)),),
        (dispatch, cap_dual),
        arg_specs=[IN_HBM] * 2,
        scratch=(pltpu.SemaphoreType.DMA((2,)),),
    )
    twin_state = lax.ppermute(give, "reg", twin)
    (part,) = call(matrix_body, (in_vmem(tile.shape[1:], BF16),), (tile, tile_mask))
    part_in = lax.ppermute(part, "reg", twin)
    small, small_give = call(small_body, (small_like,) * 2, (invest_cost, mult, cons, caps))
    small_in = lax.ppermute(small_give, "reg", twin)
    cost_give, own, dual_var, dem = call(
        functools.partial(load_body, mine),
        (half_full, three, dual_like, dual_like),
        (cost_rate, dispatch, cap_dual, dual, demand),
        arg_specs=[IN_HBM] * 5,
        scratch=(pltpu.SemaphoreType.DMA((6,)),),
    )
    twin_cost = lax.ppermute(cost_give, "reg", twin)
    matrix, turned, const, invest, near, far, mean = call(
        functools.partial(message_body, paired),
        (in_vmem((rows, 2 * width), BF16), in_vmem((2 * width, rows), BF16), invest_like, invest_like, message, message, mean_like),
        (own, twin_state, part, part_in, small, small_in),
    )
    near_in, far_in, sums = hour_exchange(near, far, mean, paired)

    scen_count = lax.axis_size("scen")
    node_count = node_of.shape[1] * scen_count // 2
    flops = 4 * mine * hours * rows * 2 * width
    prim = cap = ()
    sent = carry = received = None
    for step in range(ITERS):
        first, last = step == 0, step + 1 == ITERS
        state = (own, twin_state) if first else (*prim, *cap)
        args = [matrix, turned, own, twin_cost, dual_var, near_in, far_in, *state]
        if not first:
            args += [dem, sent, carry, received]
        outs = [half_full] * 2
        if last:
            outs += [in_vmem((mine, hours, rows // 2))] * 2
        else:
            outs += [in_vmem((mine, hours, rows), BF16), dual_like]
            if not first:
                outs += [dual_like]
        got = call(functools.partial(primal_body, paired, first, last), outs, args, flops=flops)
        fresh = tuple(got[:2])
        if not last:
            sent, carry = got[2:4]
            received = lax.ppermute(sent, "reg", other_chip)
            if not first:
                dual_var = got[4]
            *cap, invest, near, far, mean = call(
                functools.partial(cap_body, hours_all, paired, len(sums), first),
                (half_full, half_full, invest_like, message, message, mean_like),
                (*state, *fresh, invest, const, *sums),
            )
            near_in, far_in, sums = hour_exchange(near, far, mean, paired)
            if step == ITERS // 2:
                member_like = in_vmem((sections, node_count, nscen, 128))
                hot, weighted = call(
                    member_body,
                    (member_like, member_like),
                    (node_of, scen_weight),
                    arg_specs=[IN_SMEM, IN_SMEM],
                )
            prim = fresh
            continue
        prim = fresh
        inv_keep, inv_give = call(
            functools.partial(invest_body, hours_all, len(sums)),
            (inv_half,) * 2,
            (invest, const, *sums),
        )
        inv_got = lax.ppermute(inv_give, "reg", twin)
        base, rows_give = got[2:]
        rows_got = lax.ppermute(rows_give, "reg", other_chip)
        prim_got = lax.ppermute(prim[1], "reg", twin)
        capacity_all, packed = call(
            nodes_body,
            (in_vmem((sections, nscen, width)), in_vmem((sections, node_count, width + 128))),
            (inv_keep, inv_got, weighted),
        )
        if scen_count == 2:
            packs = (packed, lax.ppermute(packed, "scen", [(0, 1), (1, 0)]))
        else:
            packs = (lax.psum(packed, "scen"),)
        dispatch_out = join(prim[0], prim_got)
        own_rows = rows // reg_count
        dual_keep, dual_give = call(
            dual_body, (in_vmem((mine, own_rows, hours)),) * 2, (base, rows_got)
        )
        dual_got = lax.ppermute(dual_give, "reg", twin)
        dual_out, capacity_out, multiplier_out = call(
            functools.partial(finish_body, len(packs)),
            (
                pltpu.HBM((nscen, own_rows, hours), F32),
                pltpu.HBM((sections, nscen, width), F32),
                pltpu.HBM((sections, nscen, width), F32),
            ),
            (dual_keep, dual_got, mult, capacity_all, hot, *packs),
            out_specs=(IN_HBM,) * 3,
            scratch=(pltpu.VMEM((sections, nscen, width), F32), pltpu.SemaphoreType.DMA((4,))),
        )
    return (
        dispatch_out,
        jnp.transpose(dual_out, (0, 2, 1)),
        by_section(capacity_out),
        by_section(multiplier_out),
    )


def solution(mesh):
    placed = (
        P("scen", "hour", "reg"),
        P(None, "reg"),
        P("hour", None, "reg"),
        P("hour", None, "reg"),
        P("scen", "hour", None),
        P("scen", "hour", "reg"),
        P("scen", "hour", None),
        P("scen", "hour", "reg"),
        P("scen", None, "reg"),
        P("scen", None, "reg"),
        P("scen", None, "reg"),
        P("scen"),
        P(None, "scen"),
    )
    return jax.shard_map(
        shards,
        mesh=mesh,
        in_specs=placed,
        out_specs=(
            P("scen", "hour", "reg"),
            P("scen", "hour", "reg"),
            P("scen", None, "reg"),
            P("scen", None, "reg"),
        ),
        check_vma=False,
    )
```

```python
import functools
import math

import jax
import jax.numpy as jnp
from jax import lax
from jax.experimental import pallas as pl
from jax.experimental.pallas import tpu as pltpu
from jax.sharding import PartitionSpec as P


ITERS = 8
RAMP_WEIGHT = 0.5
PENALTY = 1.0
STEP_PRIMAL = 0.3
STEP_INVEST = 0.5
STEP_DUAL = 0.3
STEP_CAP = 0.05

F32 = jnp.float32
BF16 = jnp.bfloat16
COL_TILE = 256
VMEM_LIMIT = 24 * 1024 * 1024

IN_VMEM = pl.BlockSpec(memory_space=pltpu.VMEM)
IN_SMEM = pl.BlockSpec(memory_space=pltpu.SMEM)
IN_HBM = pl.BlockSpec(memory_space=pltpu.HBM)


def call(body, outs, args, arg_specs=None, out_specs=None, scratch=(), aliases=None, flops=0):
    if arg_specs is not None:
        args = [
            pltpu.with_memory_space_constraint(a, pltpu.HBM) if spec is IN_HBM else a
            for a, spec in zip(args, arg_specs)
        ]
    bytes_moved = sum(a.size * a.dtype.itemsize for a in args)
    bytes_moved += sum(math.prod(o.shape) * jnp.dtype(o.dtype).itemsize for o in outs)
    return pl.pallas_call(
        body,
        out_shape=tuple(outs),
        in_specs=arg_specs or [IN_VMEM] * len(args),
        out_specs=out_specs or tuple(IN_VMEM for _ in outs),
        scratch_shapes=list(scratch),
        input_output_aliases=aliases or {},
        compiler_params=pltpu.CompilerParams(vmem_limit_bytes=VMEM_LIMIT),
        cost_estimate=pl.CostEstimate(flops=flops, bytes_accessed=bytes_moved, transcendentals=0),
    )(*args)


def shape(dims, dtype=F32):
    return jax.ShapeDtypeStruct(tuple(dims), dtype)


def in_vmem(dims, dtype=F32):
    return pltpu.VMEM(tuple(dims), dtype)


def tiles(width):
    return [
        (half, slice(at, at + COL_TILE), slice(half * width + at, half * width + at + COL_TILE))
        for half in range(2)
        for at in range(0, width, COL_TILE)
    ]


def run_copies(pairs, sems):
    copies = [pltpu.make_async_copy(a, b, sems.at[i]) for i, (a, b) in enumerate(pairs)]
    for copy in copies:
        copy.start()
    for copy in copies:
        copy.wait()


def give_body(mine, *refs):
    *sources, out, sems = refs
    core = lax.rem(lax.axis_index("reg"), 2)
    given = pl.ds((1 - core) * mine, mine)
    run_copies([(src.at[given], out.at[i]) for i, src in enumerate(sources)], sems)


def load_body(mine, cost, prim, cap, dual, dem, give, own, dual_out, dem_out, sems):
    core = lax.rem(lax.axis_index("reg"), 2)
    held = pl.ds(core * mine, mine)
    pairs = [(cost.at[pl.ds((1 - core) * mine, mine)], give)]
    targets = ((prim, own.at[0]), (cap, own.at[1]), (cost, own.at[2]), (dual, dual_out), (dem, dem_out))
    run_copies(pairs + [(src.at[held], dst) for src, dst in targets], sems)


def small_body(cost, mult, cons, capacity, own, give):
    sections = cost.shape[0]
    mine = own.shape[1]
    core = lax.rem(lax.axis_index("reg"), 2)
    for g in range(sections):
        const = cost[g:g + 1, :] + mult[g] - PENALTY * cons[g]
        for at, x in ((g, const), (sections + g, capacity[g])):
            own[at] = jnp.where(core == 0, x[:mine], x[mine:])
            give[at] = jnp.where(core == 0, x[mine:], x[:mine])


def matrix_body(tile, mask, out):
    out[...] = tile[0] * mask[0].astype(F32).astype(BF16)


def message_body(paired, own, twin, near, far, mean):
    _, mine, _, width = own.shape
    both = (own, twin)
    for s in range(mine):
        for half, cols, flat in tiles(width):
            src = both[half]
            write_message(paired, near, far, s, flat, src[1, s, :, cols], src[0, s, :, cols])
    mean[...] = near[:mine, :]


def assemble_body(part, part_in, small, small_in, matrix, turned, const, invest):
    sections, width = invest.shape[0], part.shape[1]
    for half, src, rest in ((0, part, small), (1, part_in, small_in)):
        cols = slice(half * width, (half + 1) * width)
        matrix[:, cols] = src[...]
        turned[cols, :] = src[...].T
        const[:, :, cols] = rest[:sections]
        invest[:, :, cols] = rest[sections:]


def is_odd():
    return lax.rem(lax.axis_index("hour"), 2) == 1


def write_message(paired, near, far, s, flat, c, x):
    mine = near.shape[0] // 2
    hours = x.shape[0]
    hour_sum = jnp.sum(c, axis=0, keepdims=True)
    near[pl.ds(s, 1), flat] = hour_sum
    far[pl.ds(s, 1), flat] = hour_sum
    first, last = x[0:1], x[hours - 1:hours]
    if paired:
        odd = is_odd()
        first, last = jnp.where(odd, last, first), jnp.where(odd, first, last)
    near[pl.ds(mine + s, 1), flat] = last
    far[pl.ds(mine + s, 1), flat] = first


def new_invest(hours_all, sums, invest, const):
    mine = invest.shape[1]
    parts = [part[:mine, :] for part in sums]
    if len(parts) > 1:
        place = lax.axis_index("hour")
        at_end = jnp.logical_or(place == 0, place == lax.axis_size("hour") - 1)
        parts[3:] = [jnp.where(at_end, parts[4], parts[3])]
    while len(parts) > 1:
        parts = [u + v for u, v in zip(parts[0::2], parts[1::2])]
    mean = parts[0] / hours_all
    olds = [invest[g] for g in range(invest.shape[0])]
    news = [
        jnp.maximum(old - STEP_INVEST * (const[g] + PENALTY * old - mean), 0.0)
        for g, old in enumerate(olds)
    ]
    return olds, news


def invest_body(hours_all, sums_count, *refs):
    invest, const = refs[:2]
    keep, give = refs[2 + sums_count:]
    width = keep.shape[2]
    for g, new in enumerate(new_invest(hours_all, refs[2:2 + sums_count], invest, const)[1]):
        keep[g] = new[:, :width]
        give[g] = new[:, width:]


def patch(x, rows, at, hours):
    start = at // 8 * 8
    row = lax.broadcasted_iota(jnp.int32, (8, x.shape[1]), 0)
    pieces = []
    for s in range(rows.shape[0]):
        base = s * hours
        pieces.append(x[base:base + start])
        pieces.append(jnp.where(row == at - start, rows[s:s + 1], x[base + start:base + start + 8]))
        pieces.append(x[base + start + 8:base + hours])
    return jnp.concatenate([p for p in pieces if p.shape[0]], axis=0)


def primal_body(paired, first, last, *refs):
    refs = list(refs)
    take = lambda count: [refs.pop(0) for _ in range(count)]
    matrix, turned, own, twin_cost, dual, near, far = take(7)
    cost = (own.at[2], twin_cost)
    if first:
        both = take(2)
        prim, cap = [src.at[0] for src in both], [src.at[1] for src in both]
    else:
        prim, cap = take(2), take(2)
        dem, sent, carry, received = take(4)
    prim_out = take(2)
    if last:
        base_out, rows_give = take(2)
    else:
        sent_out, carry_out = take(2)
        if not first:
            dual_out = take(1)[0]
    mine, hours, width = prim[0].shape
    chip = lax.axis_index("reg") // 2
    place = lax.axis_index("hour")
    has_prev = (place > 0).astype(F32)
    has_next = (place < lax.axis_size("hour") - 1).astype(F32)
    height = mine * hours
    flatten = lambda x: x.reshape(height, x.shape[-1])
    multipliers = flatten(dual[...])
    if not first:
        image = sent[...].astype(F32) + received[...].astype(F32)
        multipliers = jnp.maximum(multipliers + STEP_DUAL * flatten(dem[...] - image), 0.0)
        if not last:
            dual_out[...] = multipliers.reshape(dual_out.shape)
    low = multipliers.astype(BF16)
    before = near[mine:, :]
    after = far[mine:, :]
    if paired:
        odd = is_odd()
        before, after = jnp.where(odd, before, after), jnp.where(odd, after, before)
    before = before * has_prev
    after = after * has_next
    total = None if first else flatten(carry[...])
    for half, cols, flat in tiles(width):
        pulled = jnp.dot(low, matrix[:, flat], preferred_element_type=F32)
        x = flatten(prim[half][:, :, cols])
        prev = pltpu.roll(x, 1, 0)
        follow = pltpu.roll(x, height - 1, 0)
        prev = patch(prev, before[:, flat], 0, hours)
        follow = patch(follow, after[:, flat], hours - 1, hours)
        rough = 2.0 * x - prev - follow
        grad = flatten(cost[half][:, :, cols]) + RAMP_WEIGHT * rough - pulled
        grad = grad + flatten(cap[half][:, :, cols])
        new = jnp.maximum(x - STEP_PRIMAL * grad, 0.0)
        prim_out[half][:, :, cols] = new.reshape(mine, hours, COL_TILE)
        ext = (2.0 * new - x).astype(BF16)
        sums = jnp.dot(ext, turned[flat, :], preferred_element_type=F32)
        total = sums if total is None else total + sums
    split = lambda x: x.reshape(mine, hours, x.shape[-1])
    if last:
        rows = total.shape[1] // 2
        low_chip = chip == 0
        keep = jnp.where(low_chip, total[:, :rows], total[:, rows:])
        rows_give[...] = split(jnp.where(low_chip, total[:, rows:], total[:, :rows]))
        base = multipliers + STEP_DUAL * flatten(dem[...])
        base_out[...] = split(jnp.where(low_chip, base[:, :rows], base[:, rows:]) - STEP_DUAL * keep)
    else:
        low_sum = total.astype(BF16)
        sent_out[...] = split(low_sum.astype(F32)).astype(BF16)
        carry_out[...] = split(total - low_sum.astype(F32))


def cap_body(hours_all, paired, sums_count, first, *refs):
    refs = list(refs)
    take = lambda count: [refs.pop(0) for _ in range(count)]
    if first:
        both = take(2)
        prim, cap = [src.at[0] for src in both], [src.at[1] for src in both]
    else:
        prim, cap = take(2), take(2)
    fresh = take(2)
    invest, const = take(2)
    sums = take(sums_count)
    cap_out = take(2)
    invest_out, near_out, far_out, mean_out = take(4)
    olds, news = new_invest(hours_all, sums, invest, const)
    limits = 0.0
    for g, (old, new) in enumerate(zip(olds, news)):
        invest_out[g] = new
        limits = limits + (2.0 * new - old)
    mine, _, width = prim[0].shape
    for s in range(mine):
        limit = limits[s:s + 1, :]
        for half, cols, flat in tiles(width):
            new = fresh[half][s, :, cols]
            ext = 2.0 * new - prim[half][s, :, cols]
            c = jnp.maximum(cap[half][s, :, cols] + STEP_CAP * (ext - limit[:, flat]), 0.0)
            cap_out[half][s, :, cols] = c
            write_message(paired, near_out, far_out, s, flat, c, new)
    mean_out[...] = near_out[:mine, :]


def join_body(*refs):
    kept, got, out, sems = refs
    mine = kept.shape[0]
    core = lax.rem(lax.axis_index("reg"), 2)
    run_copies(
        [(kept, out.at[pl.ds(core * mine, mine)]), (got, out.at[pl.ds((1 - core) * mine, mine)])],
        sems,
    )


def join(kept, got):
    mine = kept.shape[0]
    return call(
        join_body,
        (shape((2 * mine,) + kept.shape[1:]),),
        (kept, got),
        out_specs=(IN_HBM,),
        scratch=(pltpu.SemaphoreType.DMA((2,)),),
    )[0]


def dual_body(base, got, keep, give):
    core = lax.rem(lax.axis_index("reg"), 2)
    mine, part = give.shape[:2]
    for s in range(mine):
        new = jnp.maximum(base[s] - STEP_DUAL * got[s], 0.0).T
        low, high = new[:part], new[part:]
        keep[s] = jnp.where(core == 0, low, high)
        give[s] = jnp.where(core == 0, high, low)


def member_body(nodes, weights, hot, weighted):
    sections, count, scens, lanes = hot.shape
    one, zero = jnp.ones((1, lanes), F32), jnp.zeros((1, lanes), F32)
    for g in range(sections):
        for n in range(count):
            for s in range(scens):
                held = jnp.where(nodes[g, s] == n, one, zero)
                hot[g, n, s:s + 1] = held
                weighted[g, n, s:s + 1] = held * weights[s]


def widen(x, width):
    return jnp.concatenate([x] * (width // x.shape[-1]), axis=-1)


def nodes_body(keep, got, weighted, capacity, packed):
    core = lax.rem(lax.axis_index("reg"), 2)
    sections, mine, width = keep.shape
    for g in range(sections):
        capacity[g, :mine] = jnp.where(core == 0, keep[g], got[g])
        capacity[g, mine:] = jnp.where(core == 0, got[g], keep[g])
        built = capacity[g]
        for n in range(packed.shape[1]):
            weight = weighted[g, n]
            packed[g, n:n + 1, :width] = jnp.sum(widen(weight, width) * built, axis=0, keepdims=True)
            packed[g, n:n + 1, width:] = jnp.sum(weight, axis=0, keepdims=True)


def finish_body(packs_count, *refs):
    kept, got, mult, capacity, hot = refs[:5]
    packs = refs[5:5 + packs_count]
    dual_out, capacity_out, mult_out, mult_new, sems = refs[5 + packs_count:]
    core = lax.rem(lax.axis_index("reg"), 2)
    sections, scens, width = capacity.shape
    mine = scens // 2
    copies = [
        pltpu.make_async_copy(kept, dual_out.at[pl.ds(core * mine, mine)], sems.at[0]),
        pltpu.make_async_copy(got, dual_out.at[pl.ds((1 - core) * mine, mine)], sems.at[1]),
        pltpu.make_async_copy(capacity, capacity_out, sems.at[2]),
        pltpu.make_async_copy(mult_new, mult_out, sems.at[3]),
    ]
    for copy in copies[:3]:
        copy.start()
    for g in range(sections):
        packed = packs[0][g]
        for other in packs[1:]:
            packed = packed + other[g]
        mass = packed[:, width:width + 1]
        average = packed[:, :width] / jnp.where(mass > 0.0, mass, 1.0)
        back = jnp.zeros((scens, width), F32)
        for n in range(packed.shape[0]):
            back = back + widen(hot[g, n], width) * average[n:n + 1]
        mult_new[g] = mult[g] + PENALTY * (capacity[g] - back)
    copies[3].start()
    for copy in copies:
        copy.wait()


def hour_exchange(near, far, mean, paired):
    count = lax.axis_size("hour")
    if not paired:
        near_in = lax.ppermute(near, "hour", [(i, (i + 1) % count) for i in range(count)])
        far_in = lax.ppermute(far, "hour", [((i + 1) % count, i) for i in range(count)])
        return near_in, far_in, (lax.psum(mean, "hour"),)
    reg_count = lax.axis_size("reg")
    partners = lambda by: [(i, i ^ by) for i in range(count)]
    place = lambda z, r: z * reg_count + r
    mirror = lambda places: [
        (place(z, r), place(count - 1 - z, r) if z in places else place(z, r ^ 1))
        for z in range(count)
        for r in range(reg_count)
    ]
    near_in = lax.ppermute(near, "hour", partners(1))
    far_in = lax.ppermute(mean, ("hour", "reg"), mirror((0, count - 1)))
    mid_in = lax.ppermute(far, ("hour", "reg"), mirror(range(1, count - 1)))
    across = lax.ppermute(mean, "hour", partners(2))
    return near_in, mid_in, (mean, near_in, across, mid_in, far_in)


def shards(
    cost_rate,
    invest_cost,
    tile,
    tile_mask,
    demand,
    dispatch,
    dual,
    cap_dual,
    capacity,
    multiplier,
    consensus,
    scen_weight,
    node_of,
):
    reg_count = lax.axis_size("reg")
    assert reg_count == 4
    paired = lax.axis_size("hour") == 4
    nscen, hours, width = dispatch.shape
    rows = dual.shape[2]
    mine = nscen // 2
    sections = capacity.shape[1]
    hours_all = float(hours * lax.axis_size("hour"))
    twin = [(i, i ^ 1) for i in range(reg_count)]
    other_chip = [(i, i ^ 2) for i in range(reg_count)]
    half_full = in_vmem((mine, hours, width))
    three = in_vmem((3, mine, hours, width))
    dual_like = in_vmem((mine, hours, rows))
    message = in_vmem((2 * mine, 2 * width))
    mean_like = in_vmem((mine, 2 * width))
    invest_like = in_vmem((sections, mine, 2 * width))
    small_like = in_vmem((2 * sections, mine, width))
    inv_half = in_vmem((sections, mine, width))
    by_section = lambda x: jnp.transpose(x, (1, 0, 2))
    mult, cons, caps = by_section(multiplier), by_section(consensus), by_section(capacity)

    (give,) = call(
        functools.partial(give_body, mine),
        (in_vmem((2, mine, hours, width)),),
        (dispatch, cap_dual),
        arg_specs=[IN_HBM] * 2,
        scratch=(pltpu.SemaphoreType.DMA((2,)),),
    )
    twin_state = lax.ppermute(give, "reg", twin)
    (part,) = call(matrix_body, (in_vmem(tile.shape[1:], BF16),), (tile, tile_mask))
    part_in = lax.ppermute(part, "reg", twin)
    small, small_give = call(small_body, (small_like,) * 2, (invest_cost, mult, cons, caps))
    small_in = lax.ppermute(small_give, "reg", twin)
    cost_give, own, dual_var, dem = call(
        functools.partial(load_body, mine),
        (half_full, three, dual_like, dual_like),
        (cost_rate, dispatch, cap_dual, dual, demand),
        arg_specs=[IN_HBM] * 5,
        scratch=(pltpu.SemaphoreType.DMA((6,)),),
    )
    twin_cost = lax.ppermute(cost_give, "reg", twin)
    near, far, mean = call(
        functools.partial(message_body, paired), (message, message, mean_like), (own, twin_state)
    )
    matrix, turned, const, invest = call(
        assemble_body,
        (in_vmem((rows, 2 * width), BF16), in_vmem((2 * width, rows), BF16), invest_like, invest_like),
        (part, part_in, small, small_in),
    )
    near_in, far_in, sums = hour_exchange(near, far, mean, paired)

    scen_count = lax.axis_size("scen")
    node_count = node_of.shape[1] * scen_count // 2
    flops = 4 * mine * hours * rows * 2 * width
    prim = cap = ()
    sent = carry = received = None
    for step in range(ITERS):
        first, last = step == 0, step + 1 == ITERS
        state = (own, twin_state) if first else (*prim, *cap)
        args = [matrix, turned, own, twin_cost, dual_var, near_in, far_in, *state]
        if not first:
            args += [dem, sent, carry, received]
        outs = [half_full] * 2
        if last:
            outs += [in_vmem((mine, hours, rows // 2))] * 2
        else:
            outs += [in_vmem((mine, hours, rows), BF16), dual_like]
            if not first:
                outs += [dual_like]
        got = call(functools.partial(primal_body, paired, first, last), outs, args, flops=flops)
        fresh = tuple(got[:2])
        if not last:
            sent, carry = got[2:4]
            received = lax.ppermute(sent, "reg", other_chip)
            if not first:
                dual_var = got[4]
            *cap, invest, near, far, mean = call(
                functools.partial(cap_body, hours_all, paired, len(sums), first),
                (half_full, half_full, invest_like, message, message, mean_like),
                (*state, *fresh, invest, const, *sums),
            )
            near_in, far_in, sums = hour_exchange(near, far, mean, paired)
            if step == ITERS // 2:
                member_like = in_vmem((sections, node_count, nscen, 128))
                hot, weighted = call(
                    member_body,
                    (member_like, member_like),
                    (node_of, scen_weight),
                    arg_specs=[IN_SMEM, IN_SMEM],
                )
            prim = fresh
            continue
        prim = fresh
        inv_keep, inv_give = call(
            functools.partial(invest_body, hours_all, len(sums)),
            (inv_half,) * 2,
            (invest, const, *sums),
        )
        inv_got = lax.ppermute(inv_give, "reg", twin)
        base, rows_give = got[2:]
        rows_got = lax.ppermute(rows_give, "reg", other_chip)
        prim_got = lax.ppermute(prim[1], "reg", twin)
        capacity_all, packed = call(
            nodes_body,
            (in_vmem((sections, nscen, width)), in_vmem((sections, node_count, width + 128))),
            (inv_keep, inv_got, weighted),
        )
        if scen_count == 2:
            packs = (packed, lax.ppermute(packed, "scen", [(0, 1), (1, 0)]))
        else:
            packs = (lax.psum(packed, "scen"),)
        dispatch_out = join(prim[0], prim_got)
        own_rows = rows // reg_count
        dual_keep, dual_give = call(
            dual_body, (in_vmem((mine, own_rows, hours)),) * 2, (base, rows_got)
        )
        dual_got = lax.ppermute(dual_give, "reg", twin)
        dual_out, capacity_out, multiplier_out = call(
            functools.partial(finish_body, len(packs)),
            (
                pltpu.HBM((nscen, own_rows, hours), F32),
                pltpu.HBM((sections, nscen, width), F32),
                pltpu.HBM((sections, nscen, width), F32),
            ),
            (dual_keep, dual_got, mult, capacity_all, hot, *packs),
            out_specs=(IN_HBM,) * 3,
            scratch=(pltpu.VMEM((sections, nscen, width), F32), pltpu.SemaphoreType.DMA((4,))),
        )
    return (
        dispatch_out,
        jnp.transpose(dual_out, (0, 2, 1)),
        by_section(capacity_out),
        by_section(multiplier_out),
    )


def solution(mesh):
    placed = (
        P("scen", "hour", "reg"),
        P(None, "reg"),
        P("hour", None, "reg"),
        P("hour", None, "reg"),
        P("scen", "hour", None),
        P("scen", "hour", "reg"),
        P("scen", "hour", None),
        P("scen", "hour", "reg"),
        P("scen", None, "reg"),
        P("scen", None, "reg"),
        P("scen", None, "reg"),
        P("scen"),
        P(None, "scen"),
    )
    return jax.shard_map(
        shards,
        mesh=mesh,
        in_specs=placed,
        out_specs=(
            P("scen", "hour", "reg"),
            P("scen", "hour", "reg"),
            P("scen", None, "reg"),
            P("scen", None, "reg"),
        ),
        check_vma=False,
    )
```
